128 devices in a mesh: seq: 64 (over x, y_lo, z, core), grp: 2 (over y_hi).
Axes of the slice: x: 4, y: 4 (y_hi: 2, y_lo: 2; y = y_hi * 2 + y_lo), z: 4, core: 2. Of those that a mesh axis runs over, the one named last changes fastest.
Arguments:
- enc_q: bfloat16 [8192, 2048], P('seq', 'grp'), may hold values from -32 to 32
- enc_k: bfloat16 [8192, 2048], P('seq', 'grp'), may hold values from -32 to 32
- enc_v: bfloat16 [8192, 2048], P('seq', 'grp'), may hold values from -6 to 6
- enc_cot: bfloat16 [8192, 2048], P('seq', 'grp'), may hold values from -1.5 to 1.5
- cross_k: bfloat16 [8192, 2048], P('seq', 'grp'), may hold values from -32 to 32
- cross_v: bfloat16 [8192, 2048], P('seq', 'grp'), may hold values from -6 to 6
- dec_q: bfloat16 [2048, 2048], P(('seq', 'grp')), may hold values from -32 to 32
- dec_cot: bfloat16 [2048, 2048], P(('seq', 'grp')), may hold values from -1.5 to 1.5
- frame_lengths: int32 [64], replicated, may hold values from 64 to 128
Outputs:
- enc_out: bfloat16 [8192, 2048], P('seq', 'grp')
- enc_dq: bfloat16 [8192, 2048], P('seq', 'grp')
- enc_dk: bfloat16 [8192, 2048], P('seq', 'grp')
- enc_dv: bfloat16 [8192, 2048], P('seq', 'grp')
- dec_out: bfloat16 [2048, 2048], P(('seq', 'grp'))
- dec_dq: bfloat16 [2048, 2048], P(('seq', 'grp'))
- cross_dk: bfloat16 [8192, 2048], P('seq', 'grp')
- cross_dv: bfloat16 [8192, 2048], P('seq', 'grp')
The draws below stay inside these ranges and needn't reach their ends.
All inputs are finite; a program needn't handle non-finite values.
Results may differ from the reference program's by a relative error of at most 0.04.
Values may be sent and summed in bfloat16 or wider, within the bound.
A program may use at most 128 MiB of HBM per device.

```python
import jax
import jax.numpy as jnp
from jax import lax

HEADS = 16
HEAD_DIM = 128
REACH = 4
FR_DEV = 128
BLOCKS = 64
FRAMES = 8192
TOKENS = 2048


def drawn(key, salt, rows):
    inner = jax.random.fold_in(key, salt)
    return jnp.clip(jax.random.normal(inner, (rows, HEADS * HEAD_DIM), jnp.float32), -6.0, 6.0)


def drawn_queries(key, salt, rows):
    content_operand = drawn(key, salt, rows)
    return content_operand.astype(jnp.bfloat16)


def drawn_keys(key, salt, rows):
    content_operand = drawn(key, salt, rows)
    return content_operand.astype(jnp.bfloat16)


def draw_enc_q(key, part):
    return drawn_queries(key, 1, FRAMES)


def draw_enc_k(key, part):
    return drawn_keys(key, 2, FRAMES)


def draw_cross_k(key, part):
    return drawn_keys(key, 3, FRAMES)


def draw_dec_q(key, part):
    return drawn_queries(key, 4, TOKENS)


def with_ends(array, own_key, least, top_value):
    longest = array.shape.index(max(array.shape))
    spots = []
    for shift in (0, 1):
        where = [jax.random.randint(jax.random.fold_in(own_key, axis), (), 0, length) for axis, length in enumerate(array.shape)]
        where[longest] = (where[longest] + shift) % array.shape[longest]
        spots.append(tuple(where))
    return array.at[spots[0]].set(least).at[spots[1]].set(top_value)


def block_levels(own_key, extent, pieces, smallest, largest):
    loudness = 1.0
    for position, blocks in pieces:
        draws = jax.random.uniform(jax.random.fold_in(jax.random.fold_in(own_key, 6), position), (blocks,), jnp.float32, smallest / len(pieces), largest / len(pieces))
        loudness = loudness * jnp.repeat(jnp.exp(draws), extent[position] // blocks).reshape((-1,) + (1,) * (len(extent) - 1 - position))
    return loudness


def normal_values(own_key, extent, scale, reach, split=(), held_as=jnp.bfloat16):
    drawn = jax.random.normal(own_key, extent, jnp.float32) * scale
    if len(split) > 0:
        drawn = block_levels(own_key, extent, split, -0.22, 0.18) * drawn
    return jnp.clip(drawn, min=-reach, max=reach).astype(held_as)


def setup_inputs(seed: int = 0) -> dict:
    streams_of = jax.random.split(jax.random.key(seed), 10)
    enc_q = draw_enc_q(jax.random.fold_in(streams_of[9], 71), 0)
    enc_k = draw_enc_k(jax.random.fold_in(streams_of[9], 71), 0)
    enc_v = normal_values(streams_of[2], (FRAMES, HEADS * HEAD_DIM), 1.0, 6.0, ((0, 64), (1, 2)))
    enc_cot = normal_values(streams_of[3], (FRAMES, HEADS * HEAD_DIM), 0.25, 1.5, ((0, 64), (1, 2)))
    cross_k = draw_cross_k(jax.random.fold_in(streams_of[9], 71), 0)
    cross_v = normal_values(streams_of[5], (FRAMES, HEADS * HEAD_DIM), 1.0, 6.0, ((0, 64), (1, 2)))
    dec_q = draw_dec_q(jax.random.fold_in(streams_of[9], 71), 0)
    dec_cot = normal_values(streams_of[7], (TOKENS, HEADS * HEAD_DIM), 0.25, 1.5, ((0, 128),))
    frame_lengths = with_ends(jax.random.randint(streams_of[8], (BLOCKS,), FR_DEV // 2, FR_DEV + 1), jax.random.fold_in(streams_of[8], 1), FR_DEV // 2, FR_DEV).astype(jnp.int32)
    return {"enc_q": enc_q, "enc_k": enc_k, "enc_v": enc_v, "enc_cot": enc_cot, "cross_k": cross_k, "cross_v": cross_v, "dec_q": dec_q, "dec_cot": dec_cot, "frame_lengths": frame_lengths}


def lowered_precision_twin(content_operand):
    return lax.optimization_barrier(content_operand.astype(jnp.bfloat16)).astype(jnp.float32)

def windows(blocks):
    padded = jnp.pad(blocks, ((REACH, REACH), (0, 0), (0, 0)))
    return jnp.concatenate([padded[offset:offset + BLOCKS] for offset in range(2 * REACH + 1)], axis=1)

def restore_frames(grads):
    parts = grads.reshape(BLOCKS, 2 * REACH + 1, FR_DEV, HEAD_DIM)
    total = jnp.zeros((BLOCKS + 2 * REACH, FR_DEV, HEAD_DIM), jnp.float32)
    for offset in range(2 * REACH + 1):
        total = total + jnp.pad(parts[:, offset], ((offset, 2 * REACH - offset), (0, 0), (0, 0)))
    return total[REACH:REACH + BLOCKS]

def encoder_head(operands, band_valid):
    query_matrix, keyblock, valueblock, output_tangent = operands
    inverse_sqrt_depth = HEAD_DIM ** (-0.5)
    query_matrix = query_matrix.astype(jnp.float32)
    output_tangent = output_tangent.astype(jnp.float32)
    lookup_operand = windows(keyblock.astype(jnp.float32))
    content_operand = windows(valueblock.astype(jnp.float32))
    attention_logits = jnp.einsum('tyf,taf->tya', query_matrix, lookup_operand) * inverse_sqrt_depth
    mask = band_valid[:, None, :]
    top = lax.optimization_barrier(jnp.max(jnp.where(mask, attention_logits, -1e+30), axis=2, keepdims=True))
    softmax_unnormalized = jnp.where(mask, jnp.exp(attention_logits - top), 0.0)
    total = lax.optimization_barrier(jnp.sum(softmax_unnormalized, axis=2, keepdims=True))
    mixture_dividend = jnp.einsum('hpx,hxm->hpm', lowered_precision_twin(softmax_unnormalized), content_operand)
    output = (mixture_dividend / total).astype(jnp.bfloat16)
    delta = lax.optimization_barrier(jnp.sum(output_tangent * output.astype(jnp.float32), axis=2, keepdims=True))
    attention_probs = softmax_unnormalized / total
    prob_gradient = jnp.einsum('tyf,taf->tya', output_tangent, content_operand)
    similarity_adjoint = lowered_precision_twin(attention_probs * (prob_gradient - delta))
    asker_cotangent_sum = (jnp.einsum('hpx,hxm->hpm', similarity_adjoint, lookup_operand) * inverse_sqrt_depth).astype(jnp.bfloat16)
    key_gradient = restore_frames(jnp.einsum('pox,pof->pxf', similarity_adjoint, query_matrix) * inverse_sqrt_depth).astype(jnp.bfloat16)
    value_gradient = restore_frames(jnp.einsum('pox,pof->pxf', lowered_precision_twin(attention_probs), output_tangent)).astype(jnp.bfloat16)
    return (output, asker_cotangent_sum, key_gradient, value_gradient)

def cross_head(operands, frame_valid):
    query_matrix, keyrow, valuerow, output_tangent = operands
    inverse_sqrt_depth = HEAD_DIM ** (-0.5)
    attention_logits = jnp.dot(query_matrix, keyrow.T, preferred_element_type=jnp.float32) * inverse_sqrt_depth
    mask = frame_valid[None, :]
    top = lax.optimization_barrier(jnp.max(jnp.where(mask, attention_logits, -1e+30), axis=1, keepdims=True))
    softmax_unnormalized = jnp.where(mask, jnp.exp(attention_logits - top), 0.0)
    total = lax.optimization_barrier(jnp.sum(softmax_unnormalized, axis=1, keepdims=True))
    mixture_dividend = jnp.dot(softmax_unnormalized.astype(jnp.bfloat16), valuerow, preferred_element_type=jnp.float32)
    output = (mixture_dividend / total).astype(jnp.bfloat16)
    delta = lax.optimization_barrier(jnp.sum(output_tangent.astype(jnp.float32) * output.astype(jnp.float32), axis=1, keepdims=True))
    attention_probs = softmax_unnormalized / total
    prob_gradient = jnp.dot(output_tangent, valuerow.T, preferred_element_type=jnp.float32)
    similarity_adjoint = (attention_probs * (prob_gradient - delta)).astype(jnp.bfloat16)
    asker_cotangent_sum = (jnp.dot(similarity_adjoint, keyrow, preferred_element_type=jnp.float32) * inverse_sqrt_depth).astype(jnp.bfloat16)
    key_gradient = (jnp.dot(similarity_adjoint.T, query_matrix, preferred_element_type=jnp.float32) * inverse_sqrt_depth).astype(jnp.bfloat16)
    value_gradient = jnp.dot(attention_probs.astype(jnp.bfloat16).T, output_tangent, preferred_element_type=jnp.float32).astype(jnp.bfloat16)
    return (output, asker_cotangent_sum, key_gradient, value_gradient)

def frame_heads(matrix):
    return matrix.reshape(BLOCKS, FR_DEV, HEADS, HEAD_DIM).transpose(2, 0, 1, 3)

def frame_rows(tensor):
    return tensor.transpose(1, 2, 0, 3).reshape(FRAMES, HEADS * HEAD_DIM)

def token_heads(matrix, rows):
    return matrix.reshape(rows, HEADS, HEAD_DIM).transpose(1, 0, 2)

def token_rows(tensor, rows):
    return tensor.transpose(1, 0, 2).reshape(rows, HEADS * HEAD_DIM)

def reference(enc_q, enc_k, enc_v, enc_cot, cross_k, cross_v, dec_q, dec_cot, frame_lengths):
    slots = jnp.arange(FR_DEV, dtype=jnp.int32)
    block_valid = slots[None, :] < frame_lengths[:, None]
    padded_valid = jnp.pad(block_valid, ((REACH, REACH), (0, 0)))
    band_valid = jnp.concatenate([padded_valid[offset:offset + BLOCKS] for offset in range(2 * REACH + 1)], axis=1)
    encoded = lax.map(lambda operands: encoder_head(operands, band_valid), (frame_heads(enc_q), frame_heads(enc_k), frame_heads(enc_v), frame_heads(enc_cot)))
    enc_out, enc_dq, enc_dk, enc_dv = [frame_rows(item) for item in encoded]
    frame_valid = block_valid.reshape(FRAMES)
    crossed = lax.map(lambda operands: cross_head(operands, frame_valid), (token_heads(dec_q, TOKENS), token_heads(cross_k, FRAMES), token_heads(cross_v, FRAMES), token_heads(dec_cot, TOKENS)))
    dec_out = token_rows(crossed[0], TOKENS)
    dec_dq = token_rows(crossed[1], TOKENS)
    cross_dk = token_rows(crossed[2], FRAMES)
    cross_dv = token_rows(crossed[3], FRAMES)
    return (enc_out, enc_dq, enc_dk, enc_dv, dec_out, dec_dq, cross_dk, cross_dv)
```

```python
import functools
import math

import jax
import jax.numpy as jnp
from jax import lax
from jax.experimental import pallas as pl
from jax.experimental.pallas import tpu as pltpu
from jax.sharding import PartitionSpec as P

HD = 128
FB = 128
TB = 16
SCALE = HD ** (-0.5)
C2 = SCALE * math.log2(math.e)
NEG = -1e30
F32 = jnp.float32
BF16 = jnp.bfloat16
MESH = pl.DeviceIdType.MESH


def nt(a, b):
    return lax.dot_general(a, b, (((1,), (1,)), ((), ())), preferred_element_type=F32)


def nn(a, b):
    return lax.dot_general(a, b, (((1,), (0,)), ((), ())), preferred_element_type=F32)


def drain(ref, sem):
    pltpu.make_async_copy(ref, ref, sem).wait()


def lanes(column, width):
    return column if width == HD else jnp.concatenate([column] * (width // HD), axis=1)


def kernel(
    G, NF, len_ref, eq, ek, ev, ec, ckh, cvh, dqh, dch,
    o_eo, o_edq, o_edk, o_edv, o_do, o_ddq, o_cdk, o_cdv,
    eqb, ecb, ekb, evb, ekT, evT, ckb, cvb, ckT, cvT, qt, ct, pbuf, sbuf, wbuf, dsbuf,
    bias, nsend, nrecv, ssend, srecv, stat, dqsend, dqrecv,
    eos, edqs, edks, edvs, eka, eva, cka, cva, gsend, grecv, cdks, cdvs, toko, tokdq,
    sem_in, sem_halo, sem_tok, sem_num, sem_st, sem_stat, sem_dq, sem_grad, sem_out, sem_send,
):
    R = G // 2
    TC = 2 * TB * G
    W = 2 * FB
    s = lax.axis_index("seq")
    g = lax.axis_index("grp")
    f = lax.div(s, G)
    r = lax.rem(s, G)
    col = pl.ds(pl.multiple_of(r * HD, HD), HD)

    def send(src, dst, ssem, rsem, ts, tg):
        pltpu.make_async_remote_copy(
            src_ref=src, dst_ref=dst, send_sem=ssem, recv_sem=rsem,
            device_id=(ts, tg), device_id_type=MESH,
        ).start()

    def cols(ref, head):
        return ref.at[:, pl.ds(pl.multiple_of(head * HD, HD), HD)]

    def rows(ref, index, size):
        return ref.at[pl.ds(pl.multiple_of(index * size, size), size), :]

    pltpu.make_async_copy(cols(ckh, r), rows(ckb, r, FB), sem_in.at[0]).start()
    pltpu.make_async_copy(cols(cvh, r), rows(cvb, r, FB), sem_in.at[1]).start()
    pltpu.make_async_copy(cols(ek, r), rows(ekb, R + r, FB), sem_in.at[2]).start()
    pltpu.make_async_copy(cols(ev, r), rows(evb, R + r, FB), sem_in.at[3]).start()
    pltpu.make_async_copy(cols(eq, r), rows(eqb, r, FB), sem_in.at[4]).start()
    pltpu.make_async_copy(cols(ec, r), rows(ecb, r, FB), sem_in.at[5]).start()
    place = r * 2 + g
    own_tok = f * (2 * G) + place
    pltpu.make_async_copy(cols(dqh, g * G + r), rows(qt, own_tok, TB), sem_tok.at[0, f]).start()
    pltpu.make_async_copy(cols(dch, g * G + r), rows(ct, own_tok, TB), sem_tok.at[1, f]).start()

    barrier = pltpu.get_barrier_semaphore()

    def greet(ts, tg):
        pl.semaphore_signal(barrier, inc=1, device_id=(ts, tg), device_id_type=MESH)

    for n in range(1, G):
        greet(f * G + lax.rem(r + n, G), g)
    for n in range(G):
        greet(f * G + n, 1 - g)
    for n in range(1, NF):
        greet(lax.rem(f + n, NF) * G + r, g)

    @pl.when(f > 0)
    def _():
        for n in range(1, G):
            greet((f - 1) * G + lax.rem(r + n, G), g)

    @pl.when(f < NF - 1)
    def _():
        for n in range(1, G):
            greet((f + 1) * G + lax.rem(r + n, G), g)

    row = lax.broadcasted_iota(jnp.int32, (FB, HD), 0)
    for blk in range(2 * G):
        gb = f * G - R + blk
        length = len_ref[jnp.clip(gb, 0, NF * G - 1)]
        length = jnp.where((gb >= 0) & (gb < NF * G), length, 0)
        bias[blk * FB:(blk + 1) * FB, :] = jnp.where(row < length, 0.0, NEG).astype(F32)
    zero = jnp.zeros((R * FB, HD), BF16)

    @pl.when(f == 0)
    def _():
        ekb[0:R * FB, :] = zero
        evb[0:R * FB, :] = zero

    @pl.when(f == NF - 1)
    def _():
        ekb[(R + G) * FB:, :] = zero
        evb[(R + G) * FB:, :] = zero

    eka[...] = jnp.zeros(eka.shape, F32)
    eva[...] = jnp.zeros(eva.shape, F32)
    cka[...] = jnp.zeros(cka.shape, F32)
    cva[...] = jnp.zeros(cva.shape, F32)

    sides = jnp.where(f > 0, 1, 0) + jnp.where(f < NF - 1, 1, 0)
    pl.semaphore_wait(barrier, (G - 1) + G + (NF - 1) + sides * (G - 1))

    for n in range(1, 2 * G):
        to = lax.rem(place + n, 2 * G)
        tr, tg = lax.div(to, 2), lax.rem(to, 2)
        send(cols(dqh, tg * G + tr), rows(qt, own_tok, TB), sem_send.at[0], sem_tok.at[0, f], f * G + tr, tg)
        send(cols(dch, tg * G + tr), rows(ct, own_tok, TB), sem_send.at[1], sem_tok.at[1, f], f * G + tr, tg)
    for n in range(1, G):
        p = lax.rem(r + n, G)
        send(cols(ckh, p), rows(ckb, r, FB), sem_send.at[2], sem_in.at[0], f * G + p, g)
        send(cols(cvh, p), rows(cvb, r, FB), sem_send.at[3], sem_in.at[1], f * G + p, g)
    for n in range(1, G):
        p = lax.rem(r + n, G)
        send(cols(ek, p), rows(ekb, R + r, FB), sem_send.at[4], sem_in.at[2], f * G + p, g)
        send(cols(eq, p), rows(eqb, r, FB), sem_send.at[6], sem_in.at[4], f * G + p, g)
        send(cols(ev, p), rows(evb, R + r, FB), sem_send.at[5], sem_in.at[3], f * G + p, g)
        send(cols(ec, p), rows(ecb, r, FB), sem_send.at[7], sem_in.at[5], f * G + p, g)
    late = lax.div(r, R)
    fh = f - 1 + 2 * late
    slot = lax.rem(r + G + R, 2 * G) * (1 - late) + (r - R) * late
    has_halo = (fh >= 0) & (fh < NF)

    @pl.when(has_halo)
    def _():
        for n in range(G):
            p = lax.rem(r + n, G)
            send(cols(ek, p), rows(ekb, slot, FB), sem_send.at[8], sem_halo.at[0, late], fh * G + p, g)
            send(cols(ev, p), rows(evb, slot, FB), sem_send.at[9], sem_halo.at[1, late], fh * G + p, g)

    drain(rows(qt, f, TC), sem_tok.at[0, f])
    drain(rows(ct, f, TC), sem_tok.at[1, f])
    for n in range(1, NF):
        to = lax.rem(f + n, NF)
        send(rows(qt, f, TC), rows(qt, f, TC), sem_send.at[10], sem_tok.at[0, f], to * G + r, g)
    for n in range(1, NF):
        to = lax.rem(f + n, NF)
        send(rows(ct, f, TC), rows(ct, f, TC), sem_send.at[11], sem_tok.at[1, f], to * G + r, g)

    row8 = lax.broadcasted_iota(jnp.int32, (8, TC), 0)

    def pack(a, b, c):
        return jnp.where(row8 == 0, a, jnp.where(row8 == 1, b, c))

    drain(ckb, sem_in.at[0])
    drain(cvb, sem_in.at[1])
    cvT[...] = cvb[...].T
    ckT[...] = ckb[...].T

    def cross_forward(t):
        q = qt[pl.ds(pl.multiple_of(t * TC, TC), TC), :]
        top = None
        for u in range(G // 2):
            part = nt(ckb[u * W:(u + 1) * W, :], q)
            part = part + lanes(bias[(R * FB) + u * W:(R * FB) + (u + 1) * W, :], TC)
            sbuf[u * W:(u + 1) * W, 0:TC] = part
            high = jnp.max(part, axis=0, keepdims=True)
            top = high if top is None else jnp.maximum(top, high)
        total = jnp.zeros((1, TC), F32)
        for u in range(G // 2):
            expo = jnp.exp2((sbuf[u * W:(u + 1) * W, 0:TC] - top) * C2)
            total = total + jnp.sum(expo, axis=0, keepdims=True)
            pbuf[t, u * W:(u + 1) * W, :] = expo.astype(BF16)
        numer = nn(cvT[...], pbuf[t])
        nsend[t] = numer.astype(BF16)
        ssend[t] = pack(top, total, total)

    cross_forward(f)
    nrecv[f] = nsend[f]
    srecv[f] = ssend[f]

    @pl.loop(1, NF)
    def _(i):
        t = lax.rem(f + i, NF)
        drain(rows(qt, t, TC), sem_tok.at[0, t])
        cross_forward(t)
        send(nsend.at[t], nrecv.at[f], sem_send.at[12], sem_num, t * G + r, g)
        send(ssend.at[t], srecv.at[f], sem_send.at[13], sem_st, t * G + r, g)

    drain(rows(ekb, 0, G * FB), sem_in.at[2])
    drain(rows(evb, 0, G * FB), sem_in.at[3])
    drain(eqb, sem_in.at[4])
    drain(ecb, sem_in.at[5])

    @pl.when(f > 0)
    def _():
        drain(rows(ekb, 0, R * FB), sem_halo.at[0, 1])
        drain(rows(evb, 0, R * FB), sem_halo.at[1, 1])

    @pl.when(f < NF - 1)
    def _():
        drain(rows(ekb, 0, R * FB), sem_halo.at[0, 0])
        drain(rows(evb, 0, R * FB), sem_halo.at[1, 0])

    ekT[...] = ekb[...].T
    evT[...] = evb[...].T

    NU = (G + 2) // 2
    urow = lax.broadcasted_iota(jnp.int32, (W, W), 0)
    ulane = lax.broadcasted_iota(jnp.int32, (W, W), 1)

    def encoder_pair(j):
        base = pl.multiple_of(j * W, W)
        q = eqb[pl.ds(base, W), :]
        cot = ecb[pl.ds(base, W), :]
        top = None
        for u in range(NU):
            at = pl.multiple_of(base + u * W, W)
            part = nt(ekb[pl.ds(at, W), :], q) + lanes(bias[pl.ds(at, W), :], W)
            if u == 0:
                part = jnp.where((urow < FB) & (ulane >= FB), NEG, part)
            if u == NU - 1:
                part = jnp.where((urow >= FB) & (ulane < FB), NEG, part)
            sbuf[u * W:(u + 1) * W, :] = part
            high = jnp.max(part, axis=0, keepdims=True)
            top = high if top is None else jnp.maximum(top, high)
        total = jnp.zeros((1, W), F32)
        for u in range(NU):
            expo = jnp.exp2((sbuf[u * W:(u + 1) * W, :] - top) * C2)
            total = total + jnp.sum(expo, axis=0, keepdims=True)
            sbuf[u * W:(u + 1) * W, :] = expo
            wbuf[u * W:(u + 1) * W, :] = expo.astype(BF16)
        numer = nn(evT[:, pl.ds(base, NU * W)], wbuf[...])
        out = (numer / total).astype(BF16).astype(F32)
        delta = jnp.sum(cot.astype(F32).T * out, axis=0, keepdims=True)
        eos[pl.ds(base, W), :] = out.T.astype(BF16)
        inv = 1.0 / total
        for u in range(NU):
            at = pl.multiple_of(base + u * W, W)
            prob = sbuf[u * W:(u + 1) * W, :] * inv
            dprob = nt(evb[pl.ds(at, W), :], cot)
            ds = (prob * (dprob - delta)).astype(BF16)
            dsbuf[u * W:(u + 1) * W, :] = ds
            eka[pl.ds(at, W), :] += nn(ds, q)
            eva[pl.ds(at, W), :] += nn(prob.astype(BF16), cot)
        dq = nn(ekT[:, pl.ds(base, NU * W)], dsbuf[...]) * SCALE
        edqs[pl.ds(base, W), :] = dq.T.astype(BF16)
        for half in range(2):
            b = 2 * j + half

            @pl.when(b != r)
            def _():
                send(rows(eos, b, FB), o_eo.at[:, col], sem_send.at[14], sem_out.at[0], f * G + b, g)
                send(rows(edqs, b, FB), o_edq.at[:, col], sem_send.at[15], sem_out.at[1], f * G + b, g)

            @pl.when(b == r)
            def _():
                pltpu.make_async_copy(rows(eos, b, FB), o_eo.at[:, col], sem_out.at[0]).start()
                pltpu.make_async_copy(rows(edqs, b, FB), o_edq.at[:, col], sem_out.at[1]).start()

    def chunk_home(src, dst, k):
        mine = pl.ds(pl.multiple_of((g * G + r) * HD, HD), HD)
        for n in range(1, 2 * G):
            to = lax.rem(place + n, 2 * G)
            tr, tg = lax.div(to, 2), lax.rem(to, 2)
            send(rows(src, to, TB), dst.at[:, mine], sem_send.at[k], sem_out.at[k - 12], f * G + tr, tg)
        pltpu.make_async_copy(rows(src, place, TB), dst.at[:, mine], sem_out.at[k - 12]).start()

    encoder_pair(0)

    drain(nrecv.at[0:NF - 1], sem_num)
    drain(srecv.at[0:NF - 1], sem_st)
    top = srecv[0, 0:1, :]
    for n in range(1, NF):
        top = jnp.maximum(top, srecv[n, 0:1, :])
    total = jnp.zeros((1, TC), F32)
    numer = jnp.zeros((HD, TC), F32)
    for n in range(NF):
        share = jnp.exp2((srecv[n, 0:1, :] - top) * C2)
        total = total + share * srecv[n, 1:2, :]
        numer = numer + share * nrecv[n].astype(F32)
    out = (numer / total).astype(BF16).astype(F32)
    cot = ct[pl.ds(pl.multiple_of(f * TC, TC), TC), :]
    delta = jnp.sum(cot.astype(F32).T * out, axis=0, keepdims=True)
    toko[...] = out.T.astype(BF16)
    stat[f] = pack(top, 1.0 / total, delta)
    for n in range(1, NF):
        to = lax.rem(f + n, NF)
        send(stat.at[f], stat.at[f], sem_send.at[18], sem_stat.at[f], to * G + r, g)
    chunk_home(toko, o_do, 16)

    @pl.loop(1, G // 2)
    def _(j):
        encoder_pair(j)

    @pl.when(f > 0)
    def _():
        gsend[0, 0] = (eka[0:R * FB, :] * SCALE).astype(BF16)
        gsend[0, 1] = eva[0:R * FB, :].astype(BF16)
        send(gsend.at[0], grecv.at[1], sem_send.at[19], sem_grad.at[1], (f - 1) * G + r, g)

    @pl.when(f < NF - 1)
    def _():
        gsend[1, 0] = (eka[(R + G) * FB:, :] * SCALE).astype(BF16)
        gsend[1, 1] = eva[(R + G) * FB:, :].astype(BF16)
        send(gsend.at[1], grecv.at[0], sem_send.at[20], sem_grad.at[0], (f + 1) * G + r, g)

    def cross_backward(t):
        at = pl.ds(pl.multiple_of(t * TC, TC), TC)
        q = qt[at, :]
        cot = ct[at, :]
        share = jnp.exp2((ssend[t, 0:1, :] - stat[t, 0:1, :]) * C2) * stat[t, 1:2, :]
        delta = stat[t, 2:3, :]
        for u in range(G // 2):
            here = slice(u * W, (u + 1) * W)
            prob = pbuf[t, u * W:(u + 1) * W, :].astype(F32) * share
            dprob = nt(cvb[here, :], cot)
            ds = (prob * (dprob - delta)).astype(BF16)
            dsbuf[here, 0:TC] = ds
            cka[here, :] += nn(ds, q)
            cva[here, :] += nn(prob.astype(BF16), cot)
        dqsend[t] = nn(ckT[...], dsbuf[0:G * FB, 0:TC]).astype(BF16)

    def backward_step(i):
        t = lax.rem(f + i, NF)
        drain(rows(ct, t, TC), sem_tok.at[1, t])
        drain(stat.at[t], sem_stat.at[t])
        cross_backward(t)
        send(dqsend.at[t], dqrecv.at[f], sem_send.at[21], sem_dq, t * G + r, g)

    @pl.loop(1, NF // 2 + 1)
    def _(i):
        backward_step(i)

    own = slice(R * FB, (R + G) * FB)
    edks[...] = (eka[own, :] * SCALE).astype(BF16)
    edvs[...] = eva[own, :].astype(BF16)

    @pl.when(f > 0)
    def _():
        drain(grecv.at[0], sem_grad.at[0])
        edks[0:R * FB, :] = (eka[R * FB:2 * R * FB, :] * SCALE + grecv[0, 0].astype(F32)).astype(BF16)
        edvs[0:R * FB, :] = (eva[R * FB:2 * R * FB, :] + grecv[0, 1].astype(F32)).astype(BF16)

    @pl.when(f < NF - 1)
    def _():
        drain(grecv.at[1], sem_grad.at[1])
        edks[R * FB:, :] = (eka[2 * R * FB:3 * R * FB, :] * SCALE + grecv[1, 0].astype(F32)).astype(BF16)
        edvs[R * FB:, :] = (eva[2 * R * FB:3 * R * FB, :] + grecv[1, 1].astype(F32)).astype(BF16)

    def heads_home(src, dst, ks, ko):
        for n in range(1, G):
            p = lax.rem(r + n, G)
            send(rows(src, p, FB), dst.at[:, col], sem_send.at[ks], sem_out.at[ko], f * G + p, g)
        pltpu.make_async_copy(rows(src, r, FB), dst.at[:, col], sem_out.at[ko]).start()

    heads_home(edks, o_edk, 22, 2)
    heads_home(edvs, o_edv, 23, 3)

    @pl.loop(NF // 2 + 1, NF)
    def _(i):
        backward_step(i)

    cross_backward(f)
    dqrecv[f] = dqsend[f]
    cdks[...] = (cka[...] * SCALE).astype(BF16)
    heads_home(cdks, o_cdk, 24, 6)
    cdvs[...] = cva[...].astype(BF16)
    heads_home(cdvs, o_cdv, 25, 7)
    drain(dqrecv.at[0:NF - 1], sem_dq)
    dq = dqrecv[0].astype(F32)
    for n in range(1, NF):
        dq = dq + dqrecv[n].astype(F32)
    tokdq[...] = (dq * SCALE).T.astype(BF16)
    chunk_home(tokdq, o_ddq, 17)

    for k, ref in enumerate((o_eo, o_edq, o_edk, o_edv, o_do, o_ddq, o_cdk, o_cdv)):
        drain(ref, sem_out.at[k])
    others = eqb.at[0:(G - 1) * FB, :]
    tokens = qt.at[0:(2 * G - 1) * TB, :]
    drain(tokens, sem_send.at[0])
    drain(tokens, sem_send.at[1])
    for k in (2, 3, 4, 5, 6, 7, 14, 15, 22, 23, 24, 25):
        drain(others, sem_send.at[k])

    @pl.when(has_halo)
    def _():
        drain(eqb, sem_send.at[8])
        drain(eqb, sem_send.at[9])

    drain(qt.at[0:(NF - 1) * TC, :], sem_send.at[10])
    drain(qt.at[0:(NF - 1) * TC, :], sem_send.at[11])
    drain(nrecv.at[0:NF - 1], sem_send.at[12])
    drain(srecv.at[0:NF - 1], sem_send.at[13])
    drain(tokens, sem_send.at[16])
    drain(tokens, sem_send.at[17])
    drain(srecv.at[0:NF - 1], sem_send.at[18])
    drain(nrecv.at[0:NF - 1], sem_send.at[21])

    @pl.when(f > 0)
    def _():
        drain(grecv.at[0], sem_send.at[19])

    @pl.when(f < NF - 1)
    def _():
        drain(grecv.at[1], sem_send.at[20])


def local(enc_q, enc_k, enc_v, enc_cot, cross_k, cross_v, dec_q, dec_cot, frame_lengths):
    G = enc_q.shape[1] // HD
    NF = lax.axis_size("seq") // G
    R = G // 2
    TC = 2 * TB * G
    NW = (G + 2) * FB
    frames = jax.ShapeDtypeStruct(enc_q.shape, BF16)
    tokens = jax.ShapeDtypeStruct(dec_q.shape, BF16)
    any_spec = pl.BlockSpec(memory_space=pl.ANY)
    v = pltpu.VMEM
    scratch = [
        v((G * FB, HD), BF16), v((G * FB, HD), BF16),
        v((2 * G * FB, HD), BF16), v((2 * G * FB, HD), BF16),
        v((HD, 2 * G * FB), BF16), v((HD, 2 * G * FB), BF16),
        v((G * FB, HD), BF16), v((G * FB, HD), BF16),
        v((HD, G * FB), BF16), v((HD, G * FB), BF16),
        v((NF * TC, HD), BF16), v((NF * TC, HD), BF16),
        v((NF, G * FB, TC), BF16),
        v((NW, 2 * FB), F32),
        v((NW, 2 * FB), BF16), v((NW, 2 * FB), BF16),
        v((2 * G * FB, HD), F32),
        v((NF, HD, TC), BF16), v((NF, HD, TC), BF16),
        v((NF, 8, TC), F32), v((NF, 8, TC), F32), v((NF, 8, TC), F32),
        v((NF, HD, TC), BF16), v((NF, HD, TC), BF16),
        v((G * FB, HD), BF16), v((G * FB, HD), BF16),
        v((G * FB, HD), BF16), v((G * FB, HD), BF16),
        v((2 * G * FB, HD), F32), v((2 * G * FB, HD), F32),
        v((G * FB, HD), F32), v((G * FB, HD), F32),
        v((2, 2, R * FB, HD), BF16), v((2, 2, R * FB, HD), BF16),
        v((G * FB, HD), BF16), v((G * FB, HD), BF16),
        v((TC, HD), BF16), v((TC, HD), BF16),
        pltpu.SemaphoreType.DMA((6,)),
        pltpu.SemaphoreType.DMA((2, 2)),
        pltpu.SemaphoreType.DMA((2, NF)),
        pltpu.SemaphoreType.DMA(()),
        pltpu.SemaphoreType.DMA(()),
        pltpu.SemaphoreType.DMA((NF,)),
        pltpu.SemaphoreType.DMA(()),
        pltpu.SemaphoreType.DMA((2,)),
        pltpu.SemaphoreType.DMA((8,)),
        pltpu.SemaphoreType.DMA((26,)),
    ]
    return pl.pallas_call(
        functools.partial(kernel, G, NF),
        out_shape=(frames, frames, frames, frames, tokens, tokens, frames, frames),
        in_specs=[pl.BlockSpec(memory_space=pltpu.SMEM)] + [any_spec] * 8,
        out_specs=(any_spec,) * 8,
        scratch_shapes=scratch,
        compiler_params=pltpu.CompilerParams(
            collective_id=0, has_side_effects=True, vmem_limit_bytes=48 << 20
        ),
    )(frame_lengths, enc_q, enc_k, enc_v, enc_cot, cross_k, cross_v, dec_q, dec_cot)


def solution(mesh):
    frames = P("seq", "grp")
    tokens = P(("seq", "grp"), None)
    return jax.shard_map(
        local,
        mesh=mesh,
        in_specs=(frames,) * 6 + (tokens,) * 2 + (P(),),
        out_specs=(frames,) * 4 + (tokens,) * 2 + (frames,) * 2,
        check_vma=False,
    )
```

```python
import functools
import math

import jax
import jax.numpy as jnp
from jax import lax
from jax.experimental import pallas as pl
from jax.experimental.pallas import tpu as pltpu
from jax.sharding import PartitionSpec as P

HD = 128
FB = 128
TB = 16
SCALE = HD ** (-0.5)
C2 = SCALE * math.log2(math.e)
NEG = -1e30
F32 = jnp.float32
BF16 = jnp.bfloat16
MESH = pl.DeviceIdType.MESH
VMEM_ALL = 67043328


def nt(a, b):
    return lax.dot_general(a, b, (((1,), (1,)), ((), ())), preferred_element_type=F32)


def nn(a, b):
    return lax.dot_general(a, b, (((1,), (0,)), ((), ())), preferred_element_type=F32)


def drain(ref, sem):
    pltpu.make_async_copy(ref, ref, sem).wait()


def lanes(column, width):
    return column if width == HD else jnp.concatenate([column] * (width // HD), axis=1)


def kernel(
    G, NF, len_ref, eq, ek, ev, ec, ckh, cvh, dqh, dch,
    o_eo, o_edq, o_edk, o_edv, o_do, o_ddq, o_cdk, o_cdv,
    eqb, ecb, ekb, evb, ekT, evT, ckb, cvb, ckT, cvT, qt, ct, pbuf, dbuf, sbuf, wbuf, dsbuf,
    bias, nsend, nrecv, ssend, srecv, stat, dqsend, dqrecv,
    eos, edqs, edks, edvs, eka, eva, gsend, grecv, cdks, cdvs, toko, tokdq,
    sem_in, sem_halo, sem_tok, sem_num, sem_st, sem_stat, sem_dq, sem_grad, sem_out, sem_send,
):
    R = G // 2
    TC = 2 * TB * G
    W = 2 * FB
    s = lax.axis_index("seq")
    g = lax.axis_index("grp")
    fo = lax.div(s, G)
    r = lax.rem(s, G)
    x, yl = lax.div(fo, 2), lax.rem(fo, 2)
    z, c = lax.div(r, 2), lax.rem(r, 2)
    f = 2 * x + c
    h = yl * R + z
    same = yl == c
    split = yl != c
    col = pl.ds(pl.multiple_of(h * HD, HD), HD)

    def worker(group, head):
        return (lax.div(group, 2) * 2 + lax.div(head, R)) * G + lax.rem(head, R) * 2 + lax.rem(group, 2)

    def send(src, dst, ssem, rsem, ts, tg):
        pltpu.make_async_remote_copy(
            src_ref=src, dst_ref=dst, send_sem=ssem, recv_sem=rsem,
            device_id=(ts, tg), device_id_type=MESH,
        ).start()

    def move(n, src, dst, ssem, rsem, ts, tg):
        if n > 0:
            send(src, dst, ssem, rsem, ts, tg)
            return

        @pl.when(same)
        def _():
            pltpu.make_async_copy(src, dst, rsem).start()

        @pl.when(split)
        def _():
            send(src, dst, ssem, rsem, ts, tg)

    def cols(ref, head):
        return ref.at[:, pl.ds(pl.multiple_of(head * HD, HD), HD)]

    def rows(ref, index, size):
        return ref.at[pl.ds(pl.multiple_of(index * size, size), size), :]

    barrier = pltpu.get_barrier_semaphore()

    def greet(ts, tg):
        pl.semaphore_signal(barrier, inc=1, device_id=(ts, tg), device_id_type=MESH)

    for n in range(1, NF):
        greet(worker(lax.rem(f + n, NF), h), g)
    for n in range(G):
        greet(worker(fo, lax.rem(h + n, G)), 1 - g)
        greet(f * G + lax.rem(r + n, G), 1 - g)
    for n in range(1, G):
        greet(worker(fo, lax.rem(h + n, G)), g)
        greet(f * G + lax.rem(r + n, G), g)

    @pl.when(split)
    def _():
        greet(worker(fo, h), g)
        greet(f * G + r, g)

    row = lax.broadcasted_iota(jnp.int32, (FB, HD), 0)
    for blk in range(2 * G):
        gb = f * G - R + blk
        length = len_ref[jnp.clip(gb, 0, NF * G - 1)]
        length = jnp.where((gb >= 0) & (gb < NF * G), length, 0)
        bias[blk * FB:(blk + 1) * FB, :] = jnp.where(row < length, 0.0, NEG).astype(F32)
    zero = jnp.zeros((R * FB, HD), BF16)

    @pl.when(f == 0)
    def _():
        ekb[0:R * FB, :] = zero
        evb[0:R * FB, :] = zero

    @pl.when(f == NF - 1)
    def _():
        ekb[(R + G) * FB:, :] = zero
        evb[(R + G) * FB:, :] = zero

    eka[...] = jnp.zeros(eka.shape, F32)
    eva[...] = jnp.zeros(eva.shape, F32)

    pl.semaphore_wait(barrier, 4 * G + NF - 1 - 2 * jnp.where(same, 1, 0))

    place = r * 2 + g
    own_tok = fo * (2 * G) + place
    for n in range(2 * G):
        to = lax.rem(h * 2 + g + n, 2 * G)
        th, tg = lax.div(to, 2), lax.rem(to, 2)
        ts = worker(fo, th)
        move(n, cols(dqh, tg * G + th), rows(qt, own_tok, TB), sem_send.at[0], sem_tok.at[0, fo], ts, tg)
        move(n, cols(dch, tg * G + th), rows(ct, own_tok, TB), sem_send.at[1], sem_tok.at[1, fo], ts, tg)

    def spread(src, dst, slot, ks, ki):
        for n in range(G):
            p = lax.rem(h + n, G)
            move(n, cols(src, p), rows(dst, slot, FB), sem_send.at[ks], sem_in.at[ki], worker(fo, p), g)

    spread(ek, ekb, R + r, 4, 2)
    spread(ev, evb, R + r, 5, 3)

    drain(rows(qt, f, TC), sem_tok.at[0, f])
    for n in range(1, NF):
        to = lax.rem(f + n, NF)
        send(rows(qt, f, TC), rows(qt, f, TC), sem_send.at[10], sem_tok.at[0, f], worker(to, h), g)
    spread(ckh, ckb, r, 2, 0)
    spread(cvh, cvb, r, 3, 1)

    drain(ekb.at[R * FB:(R + G) * FB, :], sem_in.at[2])
    drain(evb.at[R * FB:(R + G) * FB, :], sem_in.at[3])

    @pl.when(f > 0)
    def _():
        for k, ref in enumerate((ekb, evb)):
            send(
                ref.at[R * FB:2 * R * FB, :], ref.at[(R + G) * FB:(2 * R + G) * FB, :],
                sem_send.at[8 + k], sem_halo.at[k, 0], worker(f - 1, h), g,
            )

    @pl.when(f < NF - 1)
    def _():
        for k, ref in enumerate((ekb, evb)):
            send(
                ref.at[G * FB:(R + G) * FB, :], ref.at[0:R * FB, :],
                sem_send.at[26 + k], sem_halo.at[k, 1], worker(f + 1, h), g,
            )

    spread(eq, eqb, r, 6, 4)
    spread(ec, ecb, r, 7, 5)

    row8 = lax.broadcasted_iota(jnp.int32, (8, TC), 0)

    def pack(a, b, c):
        return jnp.where(row8 == 0, a, jnp.where(row8 == 1, b, c))

    drain(ckb, sem_in.at[0])
    drain(cvb, sem_in.at[1])
    drain(rows(ct, f, TC), sem_tok.at[1, f])
    for n in range(1, NF):
        to = lax.rem(f + n, NF)
        send(rows(ct, f, TC), rows(ct, f, TC), sem_send.at[11], sem_tok.at[1, f], worker(to, h), g)
    cvT[...] = cvb[...].T
    ckT[...] = ckb[...].T

    def chunk(t):
        return pl.ds(pl.multiple_of(t * TC, TC), TC)

    def cross_forward(t):
        q = qt[chunk(t), :]
        top = None
        for u in range(G // 2):
            part = nt(ckb[u * W:(u + 1) * W, :], q)
            part = part + lanes(bias[(R * FB) + u * W:(R * FB) + (u + 1) * W, :], TC)
            sbuf[u * W:(u + 1) * W, 0:TC] = part
            high = jnp.max(part, axis=0, keepdims=True)
            top = high if top is None else jnp.maximum(top, high)
        total = jnp.zeros((1, TC), F32)
        for u in range(G // 2):
            expo = jnp.exp2((sbuf[u * W:(u + 1) * W, 0:TC] - top) * C2)
            total = total + jnp.sum(expo, axis=0, keepdims=True)
            pbuf[u * W:(u + 1) * W, chunk(t)] = expo.astype(BF16)
        numer = nn(cvT[...], pbuf[:, chunk(t)])
        nsend[t] = numer.astype(BF16)
        ssend[t] = pack(top, total, total)

    cross_forward(f)
    nrecv[f] = nsend[f]
    srecv[f] = ssend[f]

    @pl.loop(1, NF)
    def _(i):
        t = lax.rem(f + i, NF)
        drain(rows(qt, t, TC), sem_tok.at[0, t])
        cross_forward(t)
        send(nsend.at[t], nrecv.at[f], sem_send.at[12], sem_num, worker(t, h), g)
        send(ssend.at[t], srecv.at[f], sem_send.at[13], sem_st, worker(t, h), g)

    drain(eqb, sem_in.at[4])
    drain(ecb, sem_in.at[5])

    @pl.when(f > 0)
    def _():
        drain(rows(ekb, 0, R * FB), sem_halo.at[0, 1])
        drain(rows(evb, 0, R * FB), sem_halo.at[1, 1])

    @pl.when(f < NF - 1)
    def _():
        drain(rows(ekb, 0, R * FB), sem_halo.at[0, 0])
        drain(rows(evb, 0, R * FB), sem_halo.at[1, 0])

    ekT[...] = ekb[...].T
    evT[...] = evb[...].T

    NU = (G + 2) // 2
    urow = lax.broadcasted_iota(jnp.int32, (W, W), 0)
    ulane = lax.broadcasted_iota(jnp.int32, (W, W), 1)

    def home(src, b, dst, ks, ko):
        away = f * G + b

        @pl.when(away != s)
        def _():
            send(rows(src, b, FB), dst.at[:, col], sem_send.at[ks], sem_out.at[ko], away, g)

        @pl.when(away == s)
        def _():
            pltpu.make_async_copy(rows(src, b, FB), dst.at[:, col], sem_out.at[ko]).start()

    def encoder_pair(j):
        base = pl.multiple_of(j * W, W)
        q = eqb[pl.ds(base, W), :]
        cot = ecb[pl.ds(base, W), :]
        top = None
        for u in range(NU):
            at = pl.multiple_of(base + u * W, W)
            part = nt(ekb[pl.ds(at, W), :], q) + lanes(bias[pl.ds(at, W), :], W)
            if u == 0:
                part = jnp.where((urow < FB) & (ulane >= FB), NEG, part)
            if u == NU - 1:
                part = jnp.where((urow >= FB) & (ulane < FB), NEG, part)
            sbuf[u * W:(u + 1) * W, :] = part
            high = jnp.max(part, axis=0, keepdims=True)
            top = high if top is None else jnp.maximum(top, high)
        total = jnp.zeros((1, W), F32)
        for u in range(NU):
            expo = jnp.exp2((sbuf[u * W:(u + 1) * W, :] - top) * C2)
            total = total + jnp.sum(expo, axis=0, keepdims=True)
            sbuf[u * W:(u + 1) * W, :] = expo
            wbuf[u * W:(u + 1) * W, :] = expo.astype(BF16)
        numer = nn(evT[:, pl.ds(base, NU * W)], wbuf[...])
        out = (numer / total).astype(BF16).astype(F32)
        delta = jnp.sum(cot.astype(F32).T * out, axis=0, keepdims=True)
        eos[pl.ds(base, W), :] = out.T.astype(BF16)
        inv = 1.0 / total
        for u in range(NU):
            at = pl.multiple_of(base + u * W, W)
            prob = sbuf[u * W:(u + 1) * W, :] * inv
            dprob = nt(evb[pl.ds(at, W), :], cot)
            ds = (prob * (dprob - delta)).astype(BF16)
            dsbuf[u * W:(u + 1) * W, :] = ds
            eka[pl.ds(at, W), :] += nn(ds, q)
            eva[pl.ds(at, W), :] += nn(prob.astype(BF16), cot)
        dq = nn(ekT[:, pl.ds(base, NU * W)], dsbuf[...]) * SCALE
        edqs[pl.ds(base, W), :] = dq.T.astype(BF16)
        for half in range(2):
            home(eos, 2 * j + half, o_eo, 14, 0)
            home(edqs, 2 * j + half, o_edq, 15, 1)

    def chunk_home(src, dst, k):
        mine = pl.ds(pl.multiple_of((g * G + h) * HD, HD), HD)
        for n in range(2 * G):
            to = lax.rem(place + n, 2 * G)
            tr, tg = lax.div(to, 2), lax.rem(to, 2)
            move(n, rows(src, to, TB), dst.at[:, mine], sem_send.at[k], sem_out.at[k - 12], f * G + tr, tg)

    def combine():
        drain(nrecv.at[0:NF - 1], sem_num)
        drain(srecv.at[0:NF - 1], sem_st)
        top = srecv[0, 0:1, :]
        for n in range(1, NF):
            top = jnp.maximum(top, srecv[n, 0:1, :])
        total = jnp.zeros((1, TC), F32)
        numer = jnp.zeros((HD, TC), F32)
        for n in range(NF):
            share = jnp.exp2((srecv[n, 0:1, :] - top) * C2)
            total = total + share * srecv[n, 1:2, :]
            numer = numer + share * nrecv[n].astype(F32)
        out = (numer / total).astype(BF16).astype(F32)
        delta = jnp.sum(ct[chunk(f), :].astype(F32).T * out, axis=0, keepdims=True)
        toko[...] = out.T.astype(BF16)
        stat[f] = pack(top, 1.0 / total, delta)
        for n in range(1, NF):
            to = lax.rem(f + n, NF)
            send(stat.at[f], stat.at[f], sem_send.at[18], sem_stat.at[f], worker(to, h), g)
        chunk_home(toko, o_do, 16)

    @pl.loop(0, G // 4)
    def _(j):
        encoder_pair(j)

    @pl.when(f > 0)
    def _():
        gsend[0, 0] = (eka[0:R * FB, :] * SCALE).astype(BF16)
        gsend[0, 1] = eva[0:R * FB, :].astype(BF16)
        send(gsend.at[0], grecv.at[1], sem_send.at[19], sem_grad.at[1], worker(f - 1, h), g)

    combine()

    @pl.loop(G // 4, G // 2)
    def _(j):
        encoder_pair(j)

    @pl.when(f < NF - 1)
    def _():
        gsend[1, 0] = (eka[(R + G) * FB:, :] * SCALE).astype(BF16)
        gsend[1, 1] = eva[(R + G) * FB:, :].astype(BF16)
        send(gsend.at[1], grecv.at[0], sem_send.at[20], sem_grad.at[0], worker(f + 1, h), g)

    def cross_backward(t):
        cot = ct[chunk(t), :]
        share = jnp.exp2((ssend[t, 0:1, :] - stat[t, 0:1, :]) * C2) * stat[t, 1:2, :]
        delta = stat[t, 2:3, :]
        for u in range(G // 2):
            here = slice(u * W, (u + 1) * W)
            prob = pbuf[here, chunk(t)].astype(F32) * share
            dprob = nt(cvb[here, :], cot)
            dbuf[here, chunk(t)] = (prob * (dprob - delta)).astype(BF16)
            pbuf[here, chunk(t)] = prob.astype(BF16)
        dqsend[t] = nn(ckT[...], dbuf[:, chunk(t)]).astype(BF16)

    @pl.loop(1, NF)
    def _(i):
        t = lax.rem(f + i, NF)
        drain(rows(ct, t, TC), sem_tok.at[1, t])
        drain(stat.at[t], sem_stat.at[t])
        cross_backward(t)
        send(dqsend.at[t], dqrecv.at[f], sem_send.at[21], sem_dq, worker(t, h), g)

    cross_backward(f)
    dqrecv[f] = dqsend[f]

    own = slice(R * FB, (R + G) * FB)
    edks[...] = (eka[own, :] * SCALE).astype(BF16)
    edvs[...] = eva[own, :].astype(BF16)

    @pl.when(f > 0)
    def _():
        drain(grecv.at[0], sem_grad.at[0])
        edks[0:R * FB, :] = (eka[R * FB:2 * R * FB, :] * SCALE + grecv[0, 0].astype(F32)).astype(BF16)
        edvs[0:R * FB, :] = (eva[R * FB:2 * R * FB, :] + grecv[0, 1].astype(F32)).astype(BF16)

    @pl.when(f < NF - 1)
    def _():
        drain(grecv.at[1], sem_grad.at[1])
        edks[R * FB:, :] = (eka[2 * R * FB:3 * R * FB, :] * SCALE + grecv[1, 0].astype(F32)).astype(BF16)
        edvs[R * FB:, :] = (eva[2 * R * FB:3 * R * FB, :] + grecv[1, 1].astype(F32)).astype(BF16)

    for n in range(G):
        b = lax.rem(r + n, G)
        home(edks, b, o_edk, 22, 2)
        home(edvs, b, o_edv, 23, 3)

    def cross_grads(n):
        u = lax.rem(z + n, G // 2)
        here = pl.ds(pl.multiple_of(u * W, W), W)
        cdks[here, :] = (nn(dbuf[here, :], qt[...]) * SCALE).astype(BF16)
        cdvs[here, :] = nn(pbuf[here, :], ct[...]).astype(BF16)
        for half in range(2):
            home(cdks, 2 * u + half, o_cdk, 24, 6)
            home(cdvs, 2 * u + half, o_cdv, 25, 7)

    @pl.loop(0, G // 4)
    def _(n):
        cross_grads(n)

    drain(dqrecv.at[0:NF - 1], sem_dq)
    dq = dqrecv[0].astype(F32)
    for n in range(1, NF):
        dq = dq + dqrecv[n].astype(F32)
    tokdq[...] = (dq * SCALE).T.astype(BF16)
    chunk_home(tokdq, o_ddq, 17)

    @pl.loop(G // 4, G // 2)
    def _(n):
        cross_grads(n)

    for k, ref in enumerate((o_eo, o_edq, o_edk, o_edv, o_do, o_ddq, o_cdk, o_cdv)):
        drain(ref, sem_out.at[k])

    def sent(kept):
        for k in (2, 3, 4, 5, 6, 7, 14, 15, 22, 23, 24, 25):
            drain(eqb.at[0:(G - kept) * FB, :], sem_send.at[k])
        for k in (0, 1, 16, 17):
            drain(qt.at[0:(2 * G - kept) * TB, :], sem_send.at[k])

    @pl.when(same)
    def _():
        sent(1)

    @pl.when(split)
    def _():
        sent(0)

    drain(qt.at[0:(NF - 1) * TC, :], sem_send.at[10])
    drain(qt.at[0:(NF - 1) * TC, :], sem_send.at[11])
    drain(nrecv.at[0:NF - 1], sem_send.at[12])
    drain(srecv.at[0:NF - 1], sem_send.at[13])
    drain(srecv.at[0:NF - 1], sem_send.at[18])
    drain(nrecv.at[0:NF - 1], sem_send.at[21])

    @pl.when(f > 0)
    def _():
        drain(rows(ekb, 0, R * FB), sem_send.at[8])
        drain(rows(evb, 0, R * FB), sem_send.at[9])
        drain(grecv.at[0], sem_send.at[19])

    @pl.when(f < NF - 1)
    def _():
        drain(rows(ekb, 0, R * FB), sem_send.at[26])
        drain(rows(evb, 0, R * FB), sem_send.at[27])
        drain(grecv.at[1], sem_send.at[20])


def finish(*refs):
    n = 8
    sources, results, held, sems = refs[:n], refs[n:2 * n], refs[2 * n:3 * n], refs[3 * n]
    for k in range(n):
        pltpu.make_async_copy(sources[k], held[k], sems.at[0, k]).start()
    for k in range(n):
        pltpu.make_async_copy(sources[k], held[k], sems.at[0, k]).wait()
        pltpu.make_async_copy(held[k], results[k], sems.at[1, k]).start()
    for k in range(n):
        pltpu.make_async_copy(held[k], results[k], sems.at[1, k]).wait()


def local(enc_q, enc_k, enc_v, enc_cot, cross_k, cross_v, dec_q, dec_cot, frame_lengths):
    G = enc_q.shape[1] // HD
    NF = lax.axis_size("seq") // G
    R = G // 2
    TC = 2 * TB * G
    NW = (G + 2) * FB
    frames = jax.ShapeDtypeStruct(enc_q.shape, BF16)
    tokens = jax.ShapeDtypeStruct(dec_q.shape, BF16)
    any_spec = pl.BlockSpec(memory_space=pl.ANY)
    v = pltpu.VMEM
    scratch = [
        v((G * FB, HD), BF16), v((G * FB, HD), BF16),
        v((2 * G * FB, HD), BF16), v((2 * G * FB, HD), BF16),
        v((HD, 2 * G * FB), BF16), v((HD, 2 * G * FB), BF16),
        v((G * FB, HD), BF16), v((G * FB, HD), BF16),
        v((HD, G * FB), BF16), v((HD, G * FB), BF16),
        v((NF * TC, HD), BF16), v((NF * TC, HD), BF16),
        v((G * FB, NF * TC), BF16), v((G * FB, NF * TC), BF16),
        v((NW, 2 * FB), F32),
        v((NW, 2 * FB), BF16), v((NW, 2 * FB), BF16),
        v((2 * G * FB, HD), F32),
        v((NF, HD, TC), BF16), v((NF, HD, TC), BF16),
        v((NF, 8, TC), F32), v((NF, 8, TC), F32), v((NF, 8, TC), F32),
        v((NF, HD, TC), BF16), v((NF, HD, TC), BF16),
        v((G * FB, HD), BF16), v((G * FB, HD), BF16),
        v((G * FB, HD), BF16), v((G * FB, HD), BF16),
        v((2 * G * FB, HD), F32), v((2 * G * FB, HD), F32),
        v((2, 2, R * FB, HD), BF16), v((2, 2, R * FB, HD), BF16),
        v((G * FB, HD), BF16), v((G * FB, HD), BF16),
        v((TC, HD), BF16), v((TC, HD), BF16),
        pltpu.SemaphoreType.DMA((6,)),
        pltpu.SemaphoreType.DMA((2, 2)),
        pltpu.SemaphoreType.DMA((2, NF)),
        pltpu.SemaphoreType.DMA(()),
        pltpu.SemaphoreType.DMA(()),
        pltpu.SemaphoreType.DMA((NF,)),
        pltpu.SemaphoreType.DMA(()),
        pltpu.SemaphoreType.DMA((2,)),
        pltpu.SemaphoreType.DMA((8,)),
        pltpu.SemaphoreType.DMA((28,)),
    ]
    shapes = (frames, frames, frames, frames, tokens, tokens, frames, frames)
    staged = pl.pallas_call(
        functools.partial(kernel, G, NF),
        out_shape=shapes,
        in_specs=[pl.BlockSpec(memory_space=pltpu.SMEM)] + [any_spec] * 8,
        out_specs=(any_spec,) * 8,
        scratch_shapes=scratch,
        compiler_params=pltpu.CompilerParams(
            collective_id=0, has_side_effects=True, vmem_limit_bytes=VMEM_ALL
        ),
    )(frame_lengths, enc_q, enc_k, enc_v, enc_cot, cross_k, cross_v, dec_q, dec_cot)
    return pl.pallas_call(
        finish,
        out_shape=shapes,
        in_specs=[any_spec] * 8,
        out_specs=(any_spec,) * 8,
        scratch_shapes=[v(item.shape, BF16) for item in shapes] + [pltpu.SemaphoreType.DMA((2, 8))],
        compiler_params=pltpu.CompilerParams(vmem_limit_bytes=VMEM_ALL),
    )(*staged)


def solution(mesh):
    frames = P("seq", "grp")
    tokens = P(("seq", "grp"), None)
    return jax.shard_map(
        local,
        mesh=mesh,
        in_specs=(frames,) * 6 + (tokens,) * 2 + (P(),),
        out_specs=(frames,) * 4 + (tokens,) * 2 + (frames,) * 2,
        check_vma=False,
    )
```

```python
import functools
import math

import jax
import jax.numpy as jnp
from jax import lax
from jax.experimental import pallas as pl
from jax.experimental.pallas import tpu as pltpu
from jax.sharding import PartitionSpec as P

HD = 128
FB = 128
TB = 16
SCALE = HD ** (-0.5)
C2 = SCALE * math.log2(math.e)
NEG = -1e30
F32 = jnp.float32
BF16 = jnp.bfloat16
MESH = pl.DeviceIdType.MESH
VMEM_ALL = 67043328


def nt(a, b):
    return lax.dot_general(a, b, (((1,), (1,)), ((), ())), preferred_element_type=F32)


def nn(a, b):
    return lax.dot_general(a, b, (((1,), (0,)), ((), ())), preferred_element_type=F32)


def drain(ref, sem):
    pltpu.make_async_copy(ref, ref, sem).wait()


def lanes(column, width):
    return column if width == HD else jnp.concatenate([column] * (width // HD), axis=1)


def kernel(
    G, NF, len_ref, eq, ek, ev, ec, ckh, cvh, dqh, dch,
    o_eo, o_edq, o_edk, o_edv, o_do, o_ddq, o_cdk, o_cdv,
    eqb, ecb, ekb, evb, ekT, evT, ckb, cvb, ckT, cvT, qt, ct, pbuf, dbuf, sbuf, wbuf, dsbuf,
    bias, nsend, nrecv, npart, numf, ssend, srecv, spart, mloc, stat, dqsend, dqrecv, dqpart, dqown,
    eos, edqs, edks, edvs, eka, eva, gsend, grecv, cdks, cdvs, toko, tokdq,
    sem_in, sem_halo, sem_tok, sem_np, sem_num, sem_st, sem_stat, sem_dq, sem_part, sem_grad, sem_out, sem_send,
):
    R = G // 2
    NX = NF // 2
    TC = 2 * TB * G
    W = 2 * FB
    s = lax.axis_index("seq")
    g = lax.axis_index("grp")
    fo = lax.div(s, G)
    r = lax.rem(s, G)
    x, yl = lax.div(fo, 2), lax.rem(fo, 2)
    z, c = lax.div(r, 2), lax.rem(r, 2)
    f = 2 * x + c
    h = yl * R + z
    same = yl == c
    split = yl != c
    col = pl.ds(pl.multiple_of(h * HD, HD), HD)

    def worker(group, head):
        return (lax.div(group, 2) * 2 + lax.div(head, R)) * G + lax.rem(head, R) * 2 + lax.rem(group, 2)

    def send(src, dst, ssem, rsem, ts, tg):
        pltpu.make_async_remote_copy(
            src_ref=src, dst_ref=dst, send_sem=ssem, recv_sem=rsem,
            device_id=(ts, tg), device_id_type=MESH,
        ).start()

    def move(n, src, dst, ssem, rsem, ts, tg):
        if n > 0:
            send(src, dst, ssem, rsem, ts, tg)
            return

        @pl.when(same)
        def _():
            pltpu.make_async_copy(src, dst, rsem).start()

        @pl.when(split)
        def _():
            send(src, dst, ssem, rsem, ts, tg)

    def cols(ref, head):
        return ref.at[:, pl.ds(pl.multiple_of(head * HD, HD), HD)]

    def rows(ref, index, size):
        return ref.at[pl.ds(pl.multiple_of(index * size, size), size), :]

    barrier = pltpu.get_barrier_semaphore()

    def greet(ts, tg):
        pl.semaphore_signal(barrier, inc=1, device_id=(ts, tg), device_id_type=MESH)

    for n in range(1, NF):
        greet(worker(lax.rem(f + n, NF), h), g)
    for n in range(G):
        greet(worker(fo, lax.rem(h + n, G)), 1 - g)
        greet(f * G + lax.rem(r + n, G), 1 - g)
    for n in range(1, G):
        greet(worker(fo, lax.rem(h + n, G)), g)
        greet(f * G + lax.rem(r + n, G), g)

    @pl.when(split)
    def _():
        greet(worker(fo, h), g)
        greet(f * G + r, g)

    row = lax.broadcasted_iota(jnp.int32, (FB, HD), 0)
    for blk in range(2 * G):
        gb = f * G - R + blk
        length = len_ref[jnp.clip(gb, 0, NF * G - 1)]
        length = jnp.where((gb >= 0) & (gb < NF * G), length, 0)
        bias[blk * FB:(blk + 1) * FB, :] = jnp.where(row < length, 0.0, NEG).astype(F32)
    zero = jnp.zeros((R * FB, HD), BF16)

    @pl.when(f == 0)
    def _():
        ekb[0:R * FB, :] = zero
        evb[0:R * FB, :] = zero

    @pl.when(f == NF - 1)
    def _():
        ekb[(R + G) * FB:, :] = zero
        evb[(R + G) * FB:, :] = zero

    eka[...] = jnp.zeros(eka.shape, F32)
    eva[...] = jnp.zeros(eva.shape, F32)

    pl.semaphore_wait(barrier, 4 * G + NF - 1 - 2 * jnp.where(same, 1, 0))

    place = r * 2 + g
    own_tok = fo * (2 * G) + place

    def tokens_out(src, dst, k):
        for n in range(2 * G):
            to = lax.rem(h * 2 + g + n, 2 * G)
            th, tg = lax.div(to, 2), lax.rem(to, 2)
            move(n, cols(src, tg * G + th), rows(dst, own_tok, TB), sem_send.at[k], sem_tok.at[k, fo], worker(fo, th), tg)

    tokens_out(dqh, qt, 0)

    def spread(src, dst, slot, ks, ki):
        for n in range(G):
            p = lax.rem(h + n, G)
            move(n, cols(src, p), rows(dst, slot, FB), sem_send.at[ks], sem_in.at[ki], worker(fo, p), g)

    spread(ckh, ckb, r, 2, 0)
    spread(cvh, cvb, r, 3, 1)

    drain(rows(qt, f, TC), sem_tok.at[0, f])
    partner = worker(2 * x + 1 - c, h)

    def same_core(i):
        return 2 * lax.rem(x + i, NX) + c

    def other_core(i):
        return 2 * lax.rem(x + i, NX) + 1 - c

    for n in range(1, NX):
        send(rows(qt, f, TC), rows(qt, f, TC), sem_send.at[10], sem_tok.at[0, f], worker(same_core(n), h), g)
    send(rows(qt, f, TC), rows(qt, f, TC), sem_send.at[29], sem_tok.at[0, f], partner, g)
    spread(ek, ekb, R + r, 4, 2)
    spread(ev, evb, R + r, 5, 3)

    row8 = lax.broadcasted_iota(jnp.int32, (8, TC), 0)

    def pack(a, b, c):
        return jnp.where(row8 == 0, a, jnp.where(row8 == 1, b, c))

    drain(ckb, sem_in.at[0])
    drain(cvb, sem_in.at[1])
    spread(eq, eqb, r, 6, 4)
    spread(ec, ecb, r, 7, 5)
    tokens_out(dch, ct, 1)
    cvT[...] = cvb[...].T
    ckT[...] = ckb[...].T

    def chunk(t):
        return pl.ds(pl.multiple_of(t * TC, TC), TC)

    def cross_forward(t):
        q = qt[chunk(t), :]
        top = None
        for u in range(G // 2):
            part = nt(ckb[u * W:(u + 1) * W, :], q)
            part = part + lanes(bias[(R * FB) + u * W:(R * FB) + (u + 1) * W, :], TC)
            sbuf[u * W:(u + 1) * W, 0:TC] = part
            high = jnp.max(part, axis=0, keepdims=True)
            top = high if top is None else jnp.maximum(top, high)
        total = jnp.zeros((1, TC), F32)
        for u in range(G // 2):
            expo = jnp.exp2((sbuf[u * W:(u + 1) * W, 0:TC] - top) * C2)
            total = total + jnp.sum(expo, axis=0, keepdims=True)
            pbuf[u * W:(u + 1) * W, chunk(t)] = expo.astype(BF16)
        mloc[t] = pack(top, total, total)
        return nn(cvT[...], pbuf[:, chunk(t)])

    numf[x] = cross_forward(f)

    def halo_out(k, ref):
        drain(ref.at[R * FB:(R + G) * FB, :], sem_in.at[2 + k])

        @pl.when(f > 0)
        def _():
            send(
                ref.at[R * FB:2 * R * FB, :], ref.at[(R + G) * FB:(2 * R + G) * FB, :],
                sem_send.at[8 + k], sem_halo.at[k, 0], worker(f - 1, h), g,
            )

        @pl.when(f < NF - 1)
        def _():
            send(
                ref.at[G * FB:(R + G) * FB, :], ref.at[0:R * FB, :],
                sem_send.at[26 + k], sem_halo.at[k, 1], worker(f + 1, h), g,
            )

    @pl.loop(1, NX)
    def _(i):
        t = same_core(i)
        drain(rows(qt, t, TC), sem_tok.at[0, t])
        send(rows(qt, t, TC), rows(qt, t, TC), sem_send.at[29], sem_tok.at[0, t], partner, g)
        numf[lax.rem(x + i, NX)] = cross_forward(t)

    halo_out(0, ekb)

    def for_partner(i):
        t = other_core(i)
        drain(rows(qt, t, TC), sem_tok.at[0, t])
        nsend[t] = cross_forward(t).astype(BF16)
        send(nsend.at[t], npart.at[t], sem_send.at[30], sem_np.at[0, t], partner, g)
        send(mloc.at[t], spart.at[t], sem_send.at[31], sem_np.at[1, t], partner, g)

    @pl.loop(0, NX // 2)
    def _(i):
        for_partner(i)

    halo_out(1, evb)

    @pl.loop(NX // 2, NX)
    def _(i):
        for_partner(i)

    def joined(i):
        t = same_core(i)
        drain(npart.at[t], sem_np.at[0, t])
        drain(spart.at[t], sem_np.at[1, t])
        top = jnp.maximum(mloc[t, 0:1, :], spart[t, 0:1, :])
        mine = jnp.exp2((mloc[t, 0:1, :] - top) * C2)
        theirs = jnp.exp2((spart[t, 0:1, :] - top) * C2)
        total = mine * mloc[t, 1:2, :] + theirs * spart[t, 1:2, :]
        numer = mine * numf[lax.rem(x + i, NX)] + theirs * npart[t].astype(F32)
        return t, numer.astype(BF16), pack(top, total, total)

    @pl.loop(1, NX)
    def _(i):
        t, numer, stats = joined(i)
        nsend[t] = numer
        ssend[t] = stats
        send(nsend.at[t], nrecv.at[x], sem_send.at[12], sem_num, worker(t, h), g)
        send(ssend.at[t], srecv.at[x], sem_send.at[13], sem_st, worker(t, h), g)

    _, nrecv[x], srecv[x] = joined(0)

    drain(eqb, sem_in.at[4])
    drain(ecb, sem_in.at[5])

    @pl.when(f > 0)
    def _():
        drain(rows(ekb, 0, R * FB), sem_halo.at[0, 1])
        drain(rows(evb, 0, R * FB), sem_halo.at[1, 1])

    @pl.when(f < NF - 1)
    def _():
        drain(rows(ekb, 0, R * FB), sem_halo.at[0, 0])
        drain(rows(evb, 0, R * FB), sem_halo.at[1, 0])

    drain(rows(ct, f, TC), sem_tok.at[1, f])
    for n in range(1, NF):
        to = lax.rem(f + n, NF)
        send(rows(ct, f, TC), rows(ct, f, TC), sem_send.at[11], sem_tok.at[1, f], worker(to, h), g)
    ekT[...] = ekb[...].T
    evT[...] = evb[...].T

    NU = (G + 2) // 2
    urow = lax.broadcasted_iota(jnp.int32, (W, W), 0)
    ulane = lax.broadcasted_iota(jnp.int32, (W, W), 1)

    def home(src, b, dst, ks, ko):
        away = f * G + b

        @pl.when(away != s)
        def _():
            send(rows(src, b, FB), dst.at[:, col], sem_send.at[ks], sem_out.at[ko], away, g)

        @pl.when(away == s)
        def _():
            pltpu.make_async_copy(rows(src, b, FB), dst.at[:, col], sem_out.at[ko]).start()

    def encoder_pair(j):
        base = pl.multiple_of(j * W, W)
        q = eqb[pl.ds(base, W), :]
        cot = ecb[pl.ds(base, W), :]
        top = None
        for u in range(NU):
            at = pl.multiple_of(base + u * W, W)
            part = nt(ekb[pl.ds(at, W), :], q) + lanes(bias[pl.ds(at, W), :], W)
            if u == 0:
                part = jnp.where((urow < FB) & (ulane >= FB), NEG, part)
            if u == NU - 1:
                part = jnp.where((urow >= FB) & (ulane < FB), NEG, part)
            sbuf[u * W:(u + 1) * W, :] = part
            high = jnp.max(part, axis=0, keepdims=True)
            top = high if top is None else jnp.maximum(top, high)
        total = jnp.zeros((1, W), F32)
        for u in range(NU):
            expo = jnp.exp2((sbuf[u * W:(u + 1) * W, :] - top) * C2)
            total = total + jnp.sum(expo, axis=0, keepdims=True)
            sbuf[u * W:(u + 1) * W, :] = expo
            wbuf[u * W:(u + 1) * W, :] = expo.astype(BF16)
        numer = nn(evT[:, pl.ds(base, NU * W)], wbuf[...])
        out = (numer / total).astype(BF16).astype(F32)
        delta = jnp.sum(cot.astype(F32).T * out, axis=0, keepdims=True)
        eos[pl.ds(base, W), :] = out.T.astype(BF16)
        inv = 1.0 / total
        for u in range(NU):
            at = pl.multiple_of(base + u * W, W)
            prob = sbuf[u * W:(u + 1) * W, :] * inv
            dprob = nt(evb[pl.ds(at, W), :], cot)
            ds = (prob * (dprob - delta)).astype(BF16)
            dsbuf[u * W:(u + 1) * W, :] = ds
            eka[pl.ds(at, W), :] += nn(ds, q)
            eva[pl.ds(at, W), :] += nn(prob.astype(BF16), cot)
        dq = nn(ekT[:, pl.ds(base, NU * W)], dsbuf[...]) * SCALE
        edqs[pl.ds(base, W), :] = dq.T.astype(BF16)
        for half in range(2):
            home(eos, 2 * j + half, o_eo, 14, 0)
            home(edqs, 2 * j + half, o_edq, 15, 1)

    def chunk_home(src, dst, k):
        mine = pl.ds(pl.multiple_of((g * G + h) * HD, HD), HD)
        for n in range(2 * G):
            to = lax.rem(place + n, 2 * G)
            tr, tg = lax.div(to, 2), lax.rem(to, 2)
            move(n, rows(src, to, TB), dst.at[:, mine], sem_send.at[k], sem_out.at[k - 12], f * G + tr, tg)

    def combine():
        drain(nrecv.at[0:NX - 1], sem_num)
        drain(srecv.at[0:NX - 1], sem_st)
        top = srecv[0, 0:1, :]
        for n in range(1, NX):
            top = jnp.maximum(top, srecv[n, 0:1, :])
        total = jnp.zeros((1, TC), F32)
        numer = jnp.zeros((HD, TC), F32)
        for n in range(NX):
            share = jnp.exp2((srecv[n, 0:1, :] - top) * C2)
            total = total + share * srecv[n, 1:2, :]
            numer = numer + share * nrecv[n].astype(F32)
        out = (numer / total).astype(BF16).astype(F32)
        delta = jnp.sum(ct[chunk(f), :].astype(F32).T * out, axis=0, keepdims=True)
        toko[...] = out.T.astype(BF16)
        stat[f] = pack(top, 1.0 / total, delta)
        for n in range(1, NF):
            to = lax.rem(f + n, NF)
            send(stat.at[f], stat.at[f], sem_send.at[18], sem_stat.at[f], worker(to, h), g)
        chunk_home(toko, o_do, 16)

    back = lax.rem(z, 2)

    def pair_at(i):
        encoder_pair(i * (1 - back) + (G // 2 - 1 - i) * back)

    def rim(side):
        to = f - 1 + 2 * side

        @pl.when((to >= 0) & (to < NF))
        def _():
            edge = pl.ds(pl.multiple_of(side * ((R + G) * FB), R * FB), R * FB)
            gsend[side, 0] = (eka[edge, :] * SCALE).astype(BF16)
            gsend[side, 1] = eva[edge, :].astype(BF16)
            send(gsend.at[side], grecv.at[1 - side], sem_send.at[19 + side], sem_grad.at[1 - side], worker(to, h), g)

    def half_home(half):
        near = f - 1 + 2 * half
        into = pl.ds(pl.multiple_of(half * (R * FB), R * FB), R * FB)
        start = pl.ds(pl.multiple_of((1 + half) * (R * FB), R * FB), R * FB)
        there = (near >= 0) & (near < NF)

        @pl.when(there)
        def _():
            drain(grecv.at[half], sem_grad.at[half])
            edks[into, :] = (eka[start, :] * SCALE + grecv[half, 0].astype(F32)).astype(BF16)
            edvs[into, :] = (eva[start, :] + grecv[half, 1].astype(F32)).astype(BF16)

        @pl.when(jnp.logical_not(there))
        def _():
            edks[into, :] = (eka[start, :] * SCALE).astype(BF16)
            edvs[into, :] = eva[start, :].astype(BF16)

        for n in range(R):
            b = half * R + lax.rem(r + n, R)
            home(edks, b, o_edk, 22, 2)
            home(edvs, b, o_edv, 23, 3)

    @pl.loop(0, G // 4)
    def _(i):
        pair_at(i)

    rim(back)
    combine()

    @pl.loop(G // 4, G // 2)
    def _(i):
        pair_at(i)

    rim(1 - back)
    half_home(1 - back)

    def cross_backward(t):
        cot = ct[chunk(t), :]
        share = jnp.exp2((mloc[t, 0:1, :] - stat[t, 0:1, :]) * C2) * stat[t, 1:2, :]
        delta = stat[t, 2:3, :]
        for u in range(G // 2):
            here = slice(u * W, (u + 1) * W)
            prob = pbuf[here, chunk(t)].astype(F32) * share
            dprob = nt(cvb[here, :], cot)
            dbuf[here, chunk(t)] = (prob * (dprob - delta)).astype(BF16)
            pbuf[here, chunk(t)] = prob.astype(BF16)
        return nn(ckT[...], dbuf[:, chunk(t)])

    def backward_step(t):
        drain(rows(ct, t, TC), sem_tok.at[1, t])
        drain(stat.at[t], sem_stat.at[t])
        return cross_backward(t)

    @pl.loop(0, NX)
    def _(i):
        t = other_core(i)
        dqsend[t] = backward_step(t).astype(BF16)
        send(dqsend.at[t], dqpart.at[t], sem_send.at[28], sem_part.at[t], partner, g)

    @pl.loop(1, NX)
    def _(i):
        t = same_core(i)
        dq = backward_step(t)
        drain(dqpart.at[t], sem_part.at[t])
        dqsend[t] = (dq + dqpart[t].astype(F32)).astype(BF16)
        send(dqsend.at[t], dqrecv.at[x], sem_send.at[21], sem_dq, worker(t, h), g)

    half_home(back)
    dqown[...] = cross_backward(f)

    def cross_grads(n):
        u = lax.rem(z + n, G // 2)
        here = pl.ds(pl.multiple_of(u * W, W), W)
        cdks[here, :] = (nn(dbuf[here, :], qt[...]) * SCALE).astype(BF16)
        cdvs[here, :] = nn(pbuf[here, :], ct[...]).astype(BF16)
        for half in range(2):
            home(cdks, 2 * u + half, o_cdk, 24, 6)
            home(cdvs, 2 * u + half, o_cdv, 25, 7)

    @pl.loop(0, G // 4)
    def _(n):
        cross_grads(n)

    drain(dqpart.at[f], sem_part.at[f])
    drain(dqrecv.at[0:NX - 1], sem_dq)
    dq = dqown[...] + dqpart[f].astype(F32)
    for n in range(1, NX):
        dq = dq + dqrecv[lax.rem(x + n, NX)].astype(F32)
    tokdq[...] = (dq * SCALE).T.astype(BF16)
    chunk_home(tokdq, o_ddq, 17)

    @pl.loop(G // 4, G // 2)
    def _(n):
        cross_grads(n)

    for k, ref in enumerate((o_eo, o_edq, o_edk, o_edv, o_do, o_ddq, o_cdk, o_cdv)):
        drain(ref, sem_out.at[k])

    def sent(kept):
        for k in (2, 3, 4, 5, 6, 7, 14, 15, 22, 23, 24, 25):
            drain(eqb.at[0:(G - kept) * FB, :], sem_send.at[k])
        for k in (0, 1, 16, 17):
            drain(qt.at[0:(2 * G - kept) * TB, :], sem_send.at[k])

    @pl.when(same)
    def _():
        sent(1)

    @pl.when(split)
    def _():
        sent(0)

    drain(qt.at[0:(NX - 1) * TC, :], sem_send.at[10])
    drain(qt.at[0:NX * TC, :], sem_send.at[29])
    drain(nsend.at[0:NX], sem_send.at[30])
    drain(stat.at[0:NX], sem_send.at[31])
    drain(qt.at[0:(NF - 1) * TC, :], sem_send.at[11])
    drain(nsend.at[0:NX - 1], sem_send.at[12])
    drain(stat.at[0:NX - 1], sem_send.at[13])
    drain(stat.at[0:NF - 1], sem_send.at[18])
    drain(dqrecv.at[0:NX - 1], sem_send.at[21])
    drain(dqrecv.at[0:NX], sem_send.at[28])

    @pl.when(f > 0)
    def _():
        drain(rows(ekb, 0, R * FB), sem_send.at[8])
        drain(rows(evb, 0, R * FB), sem_send.at[9])
        drain(grecv.at[0], sem_send.at[19])

    @pl.when(f < NF - 1)
    def _():
        drain(rows(ekb, 0, R * FB), sem_send.at[26])
        drain(rows(evb, 0, R * FB), sem_send.at[27])
        drain(grecv.at[1], sem_send.at[20])


def finish(*refs):
    n = 8
    sources, results, held, sems = refs[:n], refs[n:2 * n], refs[2 * n:3 * n], refs[3 * n]
    for k in range(n):
        pltpu.make_async_copy(sources[k], held[k], sems.at[0, k]).start()
    for k in range(n):
        pltpu.make_async_copy(sources[k], held[k], sems.at[0, k]).wait()
        pltpu.make_async_copy(held[k], results[k], sems.at[1, k]).start()
    for k in range(n):
        pltpu.make_async_copy(held[k], results[k], sems.at[1, k]).wait()


def local(enc_q, enc_k, enc_v, enc_cot, cross_k, cross_v, dec_q, dec_cot, frame_lengths):
    G = enc_q.shape[1] // HD
    NF = lax.axis_size("seq") // G
    R = G // 2
    NX = NF // 2
    TC = 2 * TB * G
    NW = (G + 2) * FB
    frames = jax.ShapeDtypeStruct(enc_q.shape, BF16)
    tokens = jax.ShapeDtypeStruct(dec_q.shape, BF16)
    any_spec = pl.BlockSpec(memory_space=pl.ANY)
    v = pltpu.VMEM
    scratch = [
        v((G * FB, HD), BF16), v((G * FB, HD), BF16),
        v((2 * G * FB, HD), BF16), v((2 * G * FB, HD), BF16),
        v((HD, 2 * G * FB), BF16), v((HD, 2 * G * FB), BF16),
        v((G * FB, HD), BF16), v((G * FB, HD), BF16),
        v((HD, G * FB), BF16), v((HD, G * FB), BF16),
        v((NF * TC, HD), BF16), v((NF * TC, HD), BF16),
        v((G * FB, NF * TC), BF16), v((G * FB, NF * TC), BF16),
        v((NW, 2 * FB), F32),
        v((NW, 2 * FB), BF16), v((NW, 2 * FB), BF16),
        v((2 * G * FB, HD), F32),
        v((NF, HD, TC), BF16), v((NX, HD, TC), BF16),
        v((NF, HD, TC), BF16), v((NX, HD, TC), F32),
        v((NF, 8, TC), F32), v((NX, 8, TC), F32), v((NF, 8, TC), F32),
        v((NF, 8, TC), F32), v((NF, 8, TC), F32),
        v((NF, HD, TC), BF16), v((NX, HD, TC), BF16),
        v((NF, HD, TC), BF16), v((HD, TC), F32),
        v((G * FB, HD), BF16), v((G * FB, HD), BF16),
        v((G * FB, HD), BF16), v((G * FB, HD), BF16),
        v((2 * G * FB, HD), F32), v((2 * G * FB, HD), F32),
        v((2, 2, R * FB, HD), BF16), v((2, 2, R * FB, HD), BF16),
        v((G * FB, HD), BF16), v((G * FB, HD), BF16),
        v((TC, HD), BF16), v((TC, HD), BF16),
        pltpu.SemaphoreType.DMA((6,)),
        pltpu.SemaphoreType.DMA((2, 2)),
        pltpu.SemaphoreType.DMA((2, NF)),
        pltpu.SemaphoreType.DMA((2, NF)),
        pltpu.SemaphoreType.DMA(()),
        pltpu.SemaphoreType.DMA(()),
        pltpu.SemaphoreType.DMA((NF,)),
        pltpu.SemaphoreType.DMA(()),
        pltpu.SemaphoreType.DMA((NF,)),
        pltpu.SemaphoreType.DMA((2,)),
        pltpu.SemaphoreType.DMA((8,)),
        pltpu.SemaphoreType.DMA((32,)),
    ]
    shapes = (frames, frames, frames, frames, tokens, tokens, frames, frames)
    staged = pl.pallas_call(
        functools.partial(kernel, G, NF),
        out_shape=shapes,
        in_specs=[pl.BlockSpec(memory_space=pltpu.SMEM)] + [any_spec] * 8,
        out_specs=(any_spec,) * 8,
        scratch_shapes=scratch,
        compiler_params=pltpu.CompilerParams(
            collective_id=0, has_side_effects=True, vmem_limit_bytes=VMEM_ALL
        ),
    )(frame_lengths, enc_q, enc_k, enc_v, enc_cot, cross_k, cross_v, dec_q, dec_cot)
    return pl.pallas_call(
        finish,
        out_shape=shapes,
        in_specs=[any_spec] * 8,
        out_specs=(any_spec,) * 8,
        scratch_shapes=[v(item.shape, BF16) for item in shapes] + [pltpu.SemaphoreType.DMA((2, 8))],
        compiler_params=pltpu.CompilerParams(vmem_limit_bytes=VMEM_ALL),
    )(*staged)


def solution(mesh):
    frames = P("seq", "grp")
    tokens = P(("seq", "grp"), None)
    return jax.shard_map(
        local,
        mesh=mesh,
        in_specs=(frames,) * 6 + (tokens,) * 2 + (P(),),
        out_specs=(frames,) * 4 + (tokens,) * 2 + (frames,) * 2,
        check_vma=False,
    )
```

```python
import functools
import math

import jax
import jax.numpy as jnp
from jax import lax
from jax.experimental import pallas as pl
from jax.experimental.pallas import tpu as pltpu
from jax.sharding import PartitionSpec as P

HD = 128
FB = 128
TB = 16
SCALE = HD ** (-0.5)
C2 = SCALE * math.log2(math.e)
NEG = -1e30
F32 = jnp.float32
BF16 = jnp.bfloat16
MESH = pl.DeviceIdType.MESH
VMEM_ALL = 67043328


def nt(a, b):
    return lax.dot_general(a, b, (((1,), (1,)), ((), ())), preferred_element_type=F32)


def nn(a, b):
    return lax.dot_general(a, b, (((1,), (0,)), ((), ())), preferred_element_type=F32)


def drain(ref, sem):
    pltpu.make_async_copy(ref, ref, sem).wait()


def lanes(column, width):
    return column if width == HD else jnp.concatenate([column] * (width // HD), axis=1)


def kernel(
    G, NF, len_ref, eq, ek, ev, ec, ckh, cvh, dqh, dch,
    o_eo, o_edq, o_edk, o_edv, o_do, o_ddq, o_cdk, o_cdv,
    eqb, ecb, ekb, evb, ekT, evT, ckb, cvb, ckT, cvT, qt, ct, pbuf, dbuf, sbuf, sbuf2, wbuf, wbuf2, dsbuf,
    bias, nsend, nrecv, npart, numf, ssend, srecv, spart, mloc, stat, dqsend, dqrecv, dqpart, dqown,
    eos, edqs, edks, edvs, eka, eva, gsend, grecv, cdks, cdvs, toko, tokdq,
    sem_in, sem_halo, sem_tok, sem_np, sem_num, sem_st, sem_stat, sem_dq, sem_part, sem_grad, sem_out, sem_send,
):
    R = G // 2
    NX = NF // 2
    TC = 2 * TB * G
    W = 2 * FB
    s = lax.axis_index("seq")
    g = lax.axis_index("grp")
    fo = lax.div(s, G)
    r = lax.rem(s, G)
    x, yl = lax.div(fo, 2), lax.rem(fo, 2)
    z, c = lax.div(r, 2), lax.rem(r, 2)
    f = 2 * x + c
    h = yl * R + z
    same = yl == c
    split = yl != c
    col = pl.ds(pl.multiple_of(h * HD, HD), HD)

    def worker(group, head):
        return (lax.div(group, 2) * 2 + lax.div(head, R)) * G + lax.rem(head, R) * 2 + lax.rem(group, 2)

    def send(src, dst, ssem, rsem, ts, tg):
        pltpu.make_async_remote_copy(
            src_ref=src, dst_ref=dst, send_sem=ssem, recv_sem=rsem,
            device_id=(ts, tg), device_id_type=MESH,
        ).start()

    def move(n, src, dst, ssem, rsem, ts, tg):
        if n > 0:
            send(src, dst, ssem, rsem, ts, tg)
            return

        @pl.when(same)
        def _():
            pltpu.make_async_copy(src, dst, rsem).start()

        @pl.when(split)
        def _():
            send(src, dst, ssem, rsem, ts, tg)

    def cols(ref, head):
        return ref.at[:, pl.ds(pl.multiple_of(head * HD, HD), HD)]

    def rows(ref, index, size):
        return ref.at[pl.ds(pl.multiple_of(index * size, size), size), :]

    barrier = pltpu.get_barrier_semaphore()

    def greet(ts, tg):
        pl.semaphore_signal(barrier, inc=1, device_id=(ts, tg), device_id_type=MESH)

    for n in range(1, NF):
        greet(worker(lax.rem(f + n, NF), h), g)
    for n in range(G):
        greet(worker(fo, lax.rem(h + n, G)), 1 - g)
        greet(f * G + lax.rem(r + n, G), 1 - g)
    for n in range(1, G):
        greet(worker(fo, lax.rem(h + n, G)), g)
        greet(f * G + lax.rem(r + n, G), g)

    @pl.when(split)
    def _():
        greet(worker(fo, h), g)
        greet(f * G + r, g)

    row = lax.broadcasted_iota(jnp.int32, (FB, HD), 0)
    for blk in range(2 * G):
        gb = f * G - R + blk
        length = len_ref[jnp.clip(gb, 0, NF * G - 1)]
        length = jnp.where((gb >= 0) & (gb < NF * G), length, 0)
        bias[blk * FB:(blk + 1) * FB, :] = jnp.where(row < length, 0.0, NEG).astype(F32)
    zero = jnp.zeros((R * FB, HD), BF16)

    @pl.when(f == 0)
    def _():
        ekb[0:R * FB, :] = zero
        evb[0:R * FB, :] = zero

    @pl.when(f == NF - 1)
    def _():
        ekb[(R + G) * FB:, :] = zero
        evb[(R + G) * FB:, :] = zero

    eka[...] = jnp.zeros(eka.shape, F32)
    eva[...] = jnp.zeros(eva.shape, F32)

    pl.semaphore_wait(barrier, 4 * G + NF - 1 - 2 * jnp.where(same, 1, 0))

    place = r * 2 + g
    own_tok = fo * (2 * G) + place

    def tokens_out(src, dst, k):
        for n in range(2 * G):
            to = lax.rem(h * 2 + g + n, 2 * G)
            th, tg = lax.div(to, 2), lax.rem(to, 2)
            move(n, cols(src, tg * G + th), rows(dst, own_tok, TB), sem_send.at[k], sem_tok.at[k, fo], worker(fo, th), tg)

    tokens_out(dqh, qt, 0)

    def spread(src, dst, slot, ks, ki):
        for n in range(G):
            p = lax.rem(h + n, G)
            move(n, cols(src, p), rows(dst, slot, FB), sem_send.at[ks], sem_in.at[ki], worker(fo, p), g)

    spread(ckh, ckb, r, 2, 0)
    spread(cvh, cvb, r, 3, 1)

    drain(rows(qt, f, TC), sem_tok.at[0, f])
    partner = worker(2 * x + 1 - c, h)

    def same_core(i):
        return 2 * lax.rem(x + i, NX) + c

    def other_core(i):
        return 2 * lax.rem(x + i, NX) + 1 - c

    for n in range(1, NX):
        send(rows(qt, f, TC), rows(qt, f, TC), sem_send.at[10], sem_tok.at[0, f], worker(same_core(n), h), g)
    send(rows(qt, f, TC), rows(qt, f, TC), sem_send.at[29], sem_tok.at[0, f], partner, g)
    spread(ek, ekb, R + r, 4, 2)
    spread(ev, evb, R + r, 5, 3)

    row8 = lax.broadcasted_iota(jnp.int32, (8, TC), 0)

    def pack(a, b, c):
        return jnp.where(row8 == 0, a, jnp.where(row8 == 1, b, c))

    drain(ckb, sem_in.at[0])
    drain(cvb, sem_in.at[1])
    spread(eq, eqb, r, 6, 4)
    spread(ec, ecb, r, 7, 5)
    tokens_out(dch, ct, 1)
    cvT[...] = cvb[...].T
    ckT[...] = ckb[...].T

    def chunk(t):
        return pl.ds(pl.multiple_of(t * TC, TC), TC)

    def cross_forward(t):
        q = qt[chunk(t), :]
        top = None
        for u in range(G // 2):
            part = nt(ckb[u * W:(u + 1) * W, :], q)
            part = part + lanes(bias[(R * FB) + u * W:(R * FB) + (u + 1) * W, :], TC)
            sbuf[u * W:(u + 1) * W, 0:TC] = part
            high = jnp.max(part, axis=0, keepdims=True)
            top = high if top is None else jnp.maximum(top, high)
        total = jnp.zeros((1, TC), F32)
        for u in range(G // 2):
            expo = jnp.exp2((sbuf[u * W:(u + 1) * W, 0:TC] - top) * C2)
            total = total + jnp.sum(expo, axis=0, keepdims=True)
            pbuf[u * W:(u + 1) * W, chunk(t)] = expo.astype(BF16)
        mloc[t] = pack(top, total, total)
        return nn(cvT[...], pbuf[:, chunk(t)])

    numf[x] = cross_forward(f)

    def halo_out(k, ref):
        drain(ref.at[R * FB:(R + G) * FB, :], sem_in.at[2 + k])

        @pl.when(f > 0)
        def _():
            send(
                ref.at[R * FB:2 * R * FB, :], ref.at[(R + G) * FB:(2 * R + G) * FB, :],
                sem_send.at[8 + k], sem_halo.at[k, 0], worker(f - 1, h), g,
            )

        @pl.when(f < NF - 1)
        def _():
            send(
                ref.at[G * FB:(R + G) * FB, :], ref.at[0:R * FB, :],
                sem_send.at[26 + k], sem_halo.at[k, 1], worker(f + 1, h), g,
            )

    @pl.loop(1, NX)
    def _(i):
        t = same_core(i)
        drain(rows(qt, t, TC), sem_tok.at[0, t])
        send(rows(qt, t, TC), rows(qt, t, TC), sem_send.at[29], sem_tok.at[0, t], partner, g)
        numf[lax.rem(x + i, NX)] = cross_forward(t)

    halo_out(0, ekb)
    def for_partner(i):
        t = other_core(i)
        drain(rows(qt, t, TC), sem_tok.at[0, t])
        nsend[t] = cross_forward(t).astype(BF16)
        send(nsend.at[t], npart.at[t], sem_send.at[30], sem_np.at[0, t], partner, g)
        send(mloc.at[t], spart.at[t], sem_send.at[31], sem_np.at[1, t], partner, g)

    @pl.loop(0, NX // 2)
    def _(i):
        for_partner(i)

    halo_out(1, evb)

    @pl.loop(NX // 2, NX)
    def _(i):
        for_partner(i)

    def joined(i):
        t = same_core(i)
        drain(npart.at[t], sem_np.at[0, t])
        drain(spart.at[t], sem_np.at[1, t])
        top = jnp.maximum(mloc[t, 0:1, :], spart[t, 0:1, :])
        mine = jnp.exp2((mloc[t, 0:1, :] - top) * C2)
        theirs = jnp.exp2((spart[t, 0:1, :] - top) * C2)
        total = mine * mloc[t, 1:2, :] + theirs * spart[t, 1:2, :]
        numer = mine * numf[lax.rem(x + i, NX)] + theirs * npart[t].astype(F32)
        return t, numer.astype(BF16), pack(top, total, total)

    @pl.loop(1, NX)
    def _(i):
        t, numer, stats = joined(i)
        nsend[t] = numer
        ssend[t] = stats
        send(nsend.at[t], nrecv.at[x], sem_send.at[12], sem_num, worker(t, h), g)
        send(ssend.at[t], srecv.at[x], sem_send.at[13], sem_st, worker(t, h), g)

    _, nrecv[x], srecv[x] = joined(0)

    def halo_in(k, ref):
        @pl.when(f > 0)
        def _():
            drain(rows(ref, 0, R * FB), sem_halo.at[k, 1])

        @pl.when(f < NF - 1)
        def _():
            drain(rows(ref, 0, R * FB), sem_halo.at[k, 0])

    drain(eqb, sem_in.at[4])
    halo_in(0, ekb)
    ekT[...] = ekb[...].T

    NU = (G + 2) // 2
    urow = lax.broadcasted_iota(jnp.int32, (W, W), 0)
    ulane = lax.broadcasted_iota(jnp.int32, (W, W), 1)

    def home(src, b, dst, ks, ko):
        away = f * G + b

        @pl.when(away != s)
        def _():
            send(rows(src, b, FB), dst.at[:, col], sem_send.at[ks], sem_out.at[ko], away, g)

        @pl.when(away == s)
        def _():
            pltpu.make_async_copy(rows(src, b, FB), dst.at[:, col], sem_out.at[ko]).start()

    def score(j, u, sb):
        at = pl.ds(pl.multiple_of(j * W + u * W, W), W)
        q = eqb[pl.ds(pl.multiple_of(j * W, W), W), :]
        part = nt(ekb[at, :], q) + lanes(bias[at, :], W)
        if u == 0:
            part = jnp.where((urow < FB) & (ulane >= FB), NEG, part)
        if u == NU - 1:
            part = jnp.where((urow >= FB) & (ulane < FB), NEG, part)
        sb[u * W:(u + 1) * W, :] = part
        return jnp.max(part, axis=0, keepdims=True)

    def exponents(top, sb, wb):
        total = jnp.zeros((1, W), F32)
        for u in range(NU):
            expo = jnp.exp2((sb[u * W:(u + 1) * W, :] - top) * C2)
            total = total + jnp.sum(expo, axis=0, keepdims=True)
            sb[u * W:(u + 1) * W, :] = expo
            wb[u * W:(u + 1) * W, :] = expo.astype(BF16)
        return total

    def output(j, total, wb):
        base = pl.multiple_of(j * W, W)
        numer = nn(evT[:, pl.ds(base, NU * W)], wb[...])
        out = (numer / total).astype(BF16).astype(F32)
        delta = jnp.sum(ecb[pl.ds(base, W), :].astype(F32).T * out, axis=0, keepdims=True)
        eos[pl.ds(base, W), :] = out.T.astype(BF16)
        return 1.0 / total, delta

    def gradients(j, u, sb, inv, delta):
        base = pl.multiple_of(j * W, W)
        at = pl.multiple_of(base + u * W, W)
        q = eqb[pl.ds(base, W), :]
        cot = ecb[pl.ds(base, W), :]
        prob = sb[u * W:(u + 1) * W, :] * inv
        dprob = nt(evb[pl.ds(at, W), :], cot)
        ds = (prob * (dprob - delta)).astype(BF16)
        dsbuf[u * W:(u + 1) * W, :] = ds
        eka[pl.ds(at, W), :] += nn(ds, q)
        eva[pl.ds(at, W), :] += nn(prob.astype(BF16), cot)

    def pair_step(j, sb, wb, inv, delta, nj, nsb, nwb):
        base = pl.multiple_of(j * W, W)
        top = None
        for u in range(NU):
            gradients(j, u, sb, inv, delta)
            if nj is not None:
                high = score(nj, u, nsb)
                top = high if top is None else jnp.maximum(top, high)
        dq = nn(ekT[:, pl.ds(base, NU * W)], dsbuf[...]) * SCALE
        edqs[pl.ds(base, W), :] = dq.T.astype(BF16)
        ahead = None
        if nj is not None:
            total = exponents(top, nsb, nwb)
            ahead = output(nj, total, nwb)
        for half in range(2):
            home(eos, 2 * j + half, o_eo, 14, 0)
            home(edqs, 2 * j + half, o_edq, 15, 1)
        return ahead

    def chunk_home(src, dst, k):
        mine = pl.ds(pl.multiple_of((g * G + h) * HD, HD), HD)
        for n in range(2 * G):
            to = lax.rem(place + n, 2 * G)
            tr, tg = lax.div(to, 2), lax.rem(to, 2)
            move(n, rows(src, to, TB), dst.at[:, mine], sem_send.at[k], sem_out.at[k - 12], f * G + tr, tg)

    def combine():
        drain(nrecv.at[0:NX - 1], sem_num)
        drain(srecv.at[0:NX - 1], sem_st)
        top = srecv[0, 0:1, :]
        for n in range(1, NX):
            top = jnp.maximum(top, srecv[n, 0:1, :])
        total = jnp.zeros((1, TC), F32)
        numer = jnp.zeros((HD, TC), F32)
        for n in range(NX):
            share = jnp.exp2((srecv[n, 0:1, :] - top) * C2)
            total = total + share * srecv[n, 1:2, :]
            numer = numer + share * nrecv[n].astype(F32)
        out = (numer / total).astype(BF16).astype(F32)
        delta = jnp.sum(ct[chunk(f), :].astype(F32).T * out, axis=0, keepdims=True)
        toko[...] = out.T.astype(BF16)
        stat[f] = pack(top, 1.0 / total, delta)
        for n in range(1, NF):
            to = lax.rem(f + n, NF)
            send(stat.at[f], stat.at[f], sem_send.at[18], sem_stat.at[f], worker(to, h), g)
        chunk_home(toko, o_do, 16)

    back = lax.rem(z, 2)

    def pair_at(i):
        return i * (1 - back) + (G // 2 - 1 - i) * back

    def rim(side):
        to = f - 1 + 2 * side

        @pl.when((to >= 0) & (to < NF))
        def _():
            edge = pl.ds(pl.multiple_of(side * ((R + G) * FB), R * FB), R * FB)
            gsend[side, 0] = (eka[edge, :] * SCALE).astype(BF16)
            gsend[side, 1] = eva[edge, :].astype(BF16)
            send(gsend.at[side], grecv.at[1 - side], sem_send.at[19 + side], sem_grad.at[1 - side], worker(to, h), g)

    def half_home(half):
        near = f - 1 + 2 * half
        into = pl.ds(pl.multiple_of(half * (R * FB), R * FB), R * FB)
        start = pl.ds(pl.multiple_of((1 + half) * (R * FB), R * FB), R * FB)
        there = (near >= 0) & (near < NF)

        @pl.when(there)
        def _():
            drain(grecv.at[half], sem_grad.at[half])
            edks[into, :] = (eka[start, :] * SCALE + grecv[half, 0].astype(F32)).astype(BF16)
            edvs[into, :] = (eva[start, :] + grecv[half, 1].astype(F32)).astype(BF16)

        @pl.when(jnp.logical_not(there))
        def _():
            edks[into, :] = (eka[start, :] * SCALE).astype(BF16)
            edvs[into, :] = eva[start, :].astype(BF16)

        for n in range(R):
            b = half * R + lax.rem(r + n, R)
            home(edks, b, o_edk, 22, 2)
            home(edvs, b, o_edv, 23, 3)

    slots = ((sbuf, wbuf), (sbuf2, wbuf2))
    top = None
    for u in range(NU):
        high = score(pair_at(0), u, sbuf)
        top = high if top is None else jnp.maximum(top, high)
    total = exponents(top, sbuf, wbuf)
    halo_in(1, evb)
    evT[...] = evb[...].T
    drain(ecb, sem_in.at[5])
    drain(rows(ct, f, TC), sem_tok.at[1, f])
    for n in range(1, NX):
        send(rows(ct, f, TC), rows(ct, f, TC), sem_send.at[11], sem_tok.at[1, f], worker(same_core(n), h), g)
    send(rows(ct, f, TC), rows(ct, f, TC), sem_send.at[32], sem_tok.at[1, f], partner, g)
    ahead = output(pair_at(0), total, wbuf)
    for i in range(G // 2):
        if i == G // 4:
            combine()
            rim(back)
        if i == G // 2 - 1:
            for n in range(1, NX):
                t = same_core(n)
                drain(rows(ct, t, TC), sem_tok.at[1, t])
                send(rows(ct, t, TC), rows(ct, t, TC), sem_send.at[32], sem_tok.at[1, t], partner, g)
        more = i + 1 < G // 2
        ahead = pair_step(
            pair_at(i), *slots[i % 2], *ahead,
            pair_at(i + 1) if more else None, *slots[(i + 1) % 2],
        )

    rim(1 - back)

    def cross_backward(t):
        cot = ct[chunk(t), :]
        share = jnp.exp2((mloc[t, 0:1, :] - stat[t, 0:1, :]) * C2) * stat[t, 1:2, :]
        delta = stat[t, 2:3, :]
        for u in range(G // 2):
            here = slice(u * W, (u + 1) * W)
            prob = pbuf[here, chunk(t)].astype(F32) * share
            dprob = nt(cvb[here, :], cot)
            dbuf[here, chunk(t)] = (prob * (dprob - delta)).astype(BF16)
            pbuf[here, chunk(t)] = prob.astype(BF16)
        return nn(ckT[...], dbuf[:, chunk(t)])

    def backward_step(t):
        drain(stat.at[t], sem_stat.at[t])
        return cross_backward(t)

    @pl.loop(0, NX)
    def _(i):
        t = other_core(i)
        drain(rows(ct, t, TC), sem_tok.at[1, t])
        dqsend[t] = backward_step(t).astype(BF16)
        send(dqsend.at[t], dqpart.at[t], sem_send.at[28], sem_part.at[t], partner, g)

    def for_others(i):
        t = same_core(i)
        dq = backward_step(t)
        drain(dqpart.at[t], sem_part.at[t])
        dqsend[t] = (dq + dqpart[t].astype(F32)).astype(BF16)
        send(dqsend.at[t], dqrecv.at[x], sem_send.at[21], sem_dq, worker(t, h), g)

    half_home(1 - back)
    dqown[...] = cross_backward(f)

    @pl.loop(1, NX - 1)
    def _(i):
        for_others(i)

    half_home(back)
    for_others(NX - 1)

    def cross_grads(n):
        u = lax.rem(z + n, G // 2)
        here = pl.ds(pl.multiple_of(u * W, W), W)
        cdks[here, :] = (nn(dbuf[here, :], qt[...]) * SCALE).astype(BF16)
        cdvs[here, :] = nn(pbuf[here, :], ct[...]).astype(BF16)
        for half in range(2):
            home(cdks, 2 * u + half, o_cdk, 24, 6)
            home(cdvs, 2 * u + half, o_cdv, 25, 7)

    @pl.loop(0, G // 2)
    def _(n):
        cross_grads(n)

    drain(dqpart.at[f], sem_part.at[f])
    drain(dqrecv.at[0:NX - 1], sem_dq)
    dq = dqown[...] + dqpart[f].astype(F32)
    for n in range(1, NX):
        dq = dq + dqrecv[lax.rem(x + n, NX)].astype(F32)
    tokdq[...] = (dq * SCALE).T.astype(BF16)
    chunk_home(tokdq, o_ddq, 17)

    for k, ref in enumerate((o_eo, o_edq, o_edk, o_edv, o_do, o_ddq, o_cdk, o_cdv)):
        drain(ref, sem_out.at[k])

    def sent(kept):
        for k in (2, 3, 4, 5, 6, 7, 14, 15, 22, 23, 24, 25):
            drain(eqb.at[0:(G - kept) * FB, :], sem_send.at[k])
        for k in (0, 1, 16, 17):
            drain(qt.at[0:(2 * G - kept) * TB, :], sem_send.at[k])

    @pl.when(same)
    def _():
        sent(1)

    @pl.when(split)
    def _():
        sent(0)

    drain(qt.at[0:(NX - 1) * TC, :], sem_send.at[10])
    drain(qt.at[0:NX * TC, :], sem_send.at[29])
    drain(nsend.at[0:NX], sem_send.at[30])
    drain(stat.at[0:NX], sem_send.at[31])
    drain(qt.at[0:(NX - 1) * TC, :], sem_send.at[11])
    drain(qt.at[0:NX * TC, :], sem_send.at[32])
    drain(nsend.at[0:NX - 1], sem_send.at[12])
    drain(stat.at[0:NX - 1], sem_send.at[13])
    drain(stat.at[0:NF - 1], sem_send.at[18])
    drain(dqrecv.at[0:NX - 1], sem_send.at[21])
    drain(dqrecv.at[0:NX], sem_send.at[28])

    @pl.when(f > 0)
    def _():
        drain(rows(ekb, 0, R * FB), sem_send.at[8])
        drain(rows(evb, 0, R * FB), sem_send.at[9])
        drain(grecv.at[0], sem_send.at[19])

    @pl.when(f < NF - 1)
    def _():
        drain(rows(ekb, 0, R * FB), sem_send.at[26])
        drain(rows(evb, 0, R * FB), sem_send.at[27])
        drain(grecv.at[1], sem_send.at[20])


def finish(*refs):
    n = 8
    sources, results, held, sems = refs[:n], refs[n:2 * n], refs[2 * n:3 * n], refs[3 * n]
    for k in range(n):
        pltpu.make_async_copy(sources[k], held[k], sems.at[0, k]).start()
    for k in range(n):
        pltpu.make_async_copy(sources[k], held[k], sems.at[0, k]).wait()
        pltpu.make_async_copy(held[k], results[k], sems.at[1, k]).start()
    for k in range(n):
        pltpu.make_async_copy(held[k], results[k], sems.at[1, k]).wait()


def local(enc_q, enc_k, enc_v, enc_cot, cross_k, cross_v, dec_q, dec_cot, frame_lengths):
    G = enc_q.shape[1] // HD
    NF = lax.axis_size("seq") // G
    R = G // 2
    NX = NF // 2
    TC = 2 * TB * G
    NW = (G + 2) * FB
    frames = jax.ShapeDtypeStruct(enc_q.shape, BF16)
    tokens = jax.ShapeDtypeStruct(dec_q.shape, BF16)
    any_spec = pl.BlockSpec(memory_space=pl.ANY)
    v = pltpu.VMEM
    scratch = [
        v((G * FB, HD), BF16), v((G * FB, HD), BF16),
        v((2 * G * FB, HD), BF16), v((2 * G * FB, HD), BF16),
        v((HD, 2 * G * FB), BF16), v((HD, 2 * G * FB), BF16),
        v((G * FB, HD), BF16), v((G * FB, HD), BF16),
        v((HD, G * FB), BF16), v((HD, G * FB), BF16),
        v((NF * TC, HD), BF16), v((NF * TC, HD), BF16),
        v((G * FB, NF * TC), BF16), v((G * FB, NF * TC), BF16),
        v((NW, 2 * FB), F32), v((NW, 2 * FB), F32),
        v((NW, 2 * FB), BF16), v((NW, 2 * FB), BF16), v((NW, 2 * FB), BF16),
        v((2 * G * FB, HD), F32),
        v((NF, HD, TC), BF16), v((NX, HD, TC), BF16),
        v((NF, HD, TC), BF16), v((NX, HD, TC), F32),
        v((NF, 8, TC), F32), v((NX, 8, TC), F32), v((NF, 8, TC), F32),
        v((NF, 8, TC), F32), v((NF, 8, TC), F32),
        v((NF, HD, TC), BF16), v((NX, HD, TC), BF16),
        v((NF, HD, TC), BF16), v((HD, TC), F32),
        v((G * FB, HD), BF16), v((G * FB, HD), BF16),
        v((G * FB, HD), BF16), v((G * FB, HD), BF16),
        v((2 * G * FB, HD), F32), v((2 * G * FB, HD), F32),
        v((2, 2, R * FB, HD), BF16), v((2, 2, R * FB, HD), BF16),
        v((G * FB, HD), BF16), v((G * FB, HD), BF16),
        v((TC, HD), BF16), v((TC, HD), BF16),
        pltpu.SemaphoreType.DMA((6,)),
        pltpu.SemaphoreType.DMA((2, 2)),
        pltpu.SemaphoreType.DMA((2, NF)),
        pltpu.SemaphoreType.DMA((2, NF)),
        pltpu.SemaphoreType.DMA(()),
        pltpu.SemaphoreType.DMA(()),
        pltpu.SemaphoreType.DMA((NF,)),
        pltpu.SemaphoreType.DMA(()),
        pltpu.SemaphoreType.DMA((NF,)),
        pltpu.SemaphoreType.DMA((2,)),
        pltpu.SemaphoreType.DMA((8,)),
        pltpu.SemaphoreType.DMA((33,)),
    ]
    shapes = (frames, frames, frames, frames, tokens, tokens, frames, frames)
    staged = pl.pallas_call(
        functools.partial(kernel, G, NF),
        out_shape=shapes,
        in_specs=[pl.BlockSpec(memory_space=pltpu.SMEM)] + [any_spec] * 8,
        out_specs=(any_spec,) * 8,
        scratch_shapes=scratch,
        compiler_params=pltpu.CompilerParams(
            collective_id=0, has_side_effects=True, vmem_limit_bytes=VMEM_ALL
        ),
    )(frame_lengths, enc_q, enc_k, enc_v, enc_cot, cross_k, cross_v, dec_q, dec_cot)
    return pl.pallas_call(
        finish,
        out_shape=shapes,
        in_specs=[any_spec] * 8,
        out_specs=(any_spec,) * 8,
        scratch_shapes=[v(item.shape, BF16) for item in shapes] + [pltpu.SemaphoreType.DMA((2, 8))],
        compiler_params=pltpu.CompilerParams(vmem_limit_bytes=VMEM_ALL),
    )(*staged)


def solution(mesh):
    frames = P("seq", "grp")
    tokens = P(("seq", "grp"), None)
    return jax.shard_map(
        local,
        mesh=mesh,
        in_specs=(frames,) * 6 + (tokens,) * 2 + (P(),),
        out_specs=(frames,) * 4 + (tokens,) * 2 + (frames,) * 2,
        check_vma=False,
    )
```

```python
import functools
import math

import jax
import jax.numpy as jnp
from jax import lax
from jax.experimental import pallas as pl
from jax.experimental.pallas import tpu as pltpu
from jax.sharding import PartitionSpec as P

HD = 128
FB = 128
TB = 16
SCALE = HD ** (-0.5)
C2 = SCALE * math.log2(math.e)
NEG = -1e30
F32 = jnp.float32
BF16 = jnp.bfloat16
MESH = pl.DeviceIdType.MESH
VMEM_ALL = 67043328


def nt(a, b):
    return lax.dot_general(a, b, (((1,), (1,)), ((), ())), preferred_element_type=F32)


def nn(a, b):
    return lax.dot_general(a, b, (((1,), (0,)), ((), ())), preferred_element_type=F32)


def drain(ref, sem):
    pltpu.make_async_copy(ref, ref, sem).wait()


def lanes(column, width):
    return column if width == HD else jnp.concatenate([column] * (width // HD), axis=1)


def kernel(
    G, NF, len_ref, eq, ek, ev, ec, ckh, cvh, dqh, dch,
    o_eo, o_edq, o_edk, o_edv, o_do, o_ddq, o_cdk, o_cdv,
    eqb, ecb, ekb, evb, ekT, evT, ckb, cvb, ckT, cvT, qt, ct, pbuf, dbuf, sbuf, sbuf2, wbuf, wbuf2, dsbuf,
    bias, nsend, nrecv, npart, numf, ssend, srecv, spart, mloc, stat, dqsend, dqrecv, dqpart, dqown,
    eos, edqs, edks, edvs, eka, eva, gsend, grecv, cdks, cdvs, toko, tokdq,
    sem_in, sem_halo, sem_tok, sem_np, sem_num, sem_st, sem_stat, sem_dq, sem_part, sem_grad, sem_out, sem_send,
):
    R = G // 2
    NX = NF // 2
    TC = 2 * TB * G
    W = 2 * FB
    s = lax.axis_index("seq")
    g = lax.axis_index("grp")
    fo = lax.div(s, G)
    r = lax.rem(s, G)
    x, yl = lax.div(fo, 2), lax.rem(fo, 2)
    z, c = lax.div(r, 2), lax.rem(r, 2)
    f = 2 * x + c
    h = yl * R + z
    same = yl == c
    split = yl != c
    col = pl.ds(pl.multiple_of(h * HD, HD), HD)

    def worker(group, head):
        return (lax.div(group, 2) * 2 + lax.div(head, R)) * G + lax.rem(head, R) * 2 + lax.rem(group, 2)

    def send(src, dst, ssem, rsem, ts, tg):
        pltpu.make_async_remote_copy(
            src_ref=src, dst_ref=dst, send_sem=ssem, recv_sem=rsem,
            device_id=(ts, tg), device_id_type=MESH,
        ).start()

    def move(n, src, dst, ssem, rsem, ts, tg):
        if n > 0:
            send(src, dst, ssem, rsem, ts, tg)
            return

        @pl.when(same)
        def _():
            pltpu.make_async_copy(src, dst, rsem).start()

        @pl.when(split)
        def _():
            send(src, dst, ssem, rsem, ts, tg)

    def cols(ref, head):
        return ref.at[:, pl.ds(pl.multiple_of(head * HD, HD), HD)]

    def rows(ref, index, size):
        return ref.at[pl.ds(pl.multiple_of(index * size, size), size), :]

    barrier = pltpu.get_barrier_semaphore()

    def greet(ts, tg):
        pl.semaphore_signal(barrier, inc=1, device_id=(ts, tg), device_id_type=MESH)

    for n in range(1, NF):
        greet(worker(lax.rem(f + n, NF), h), g)
    for n in range(G):
        greet(worker(fo, lax.rem(h + n, G)), 1 - g)
        greet(f * G + lax.rem(r + n, G), 1 - g)
    for n in range(1, G):
        greet(worker(fo, lax.rem(h + n, G)), g)
        greet(f * G + lax.rem(r + n, G), g)

    @pl.when(split)
    def _():
        greet(worker(fo, h), g)
        greet(f * G + r, g)

    pl.semaphore_wait(barrier, 4 * G + NF - 1 - 2 * jnp.where(same, 1, 0))

    place = r * 2 + g
    own_tok = fo * (2 * G) + place

    def tokens_out(src, dst, k):
        for n in range(2 * G):
            to = lax.rem(h * 2 + g + n, 2 * G)
            th, tg = lax.div(to, 2), lax.rem(to, 2)
            move(n, cols(src, tg * G + th), rows(dst, own_tok, TB), sem_send.at[k], sem_tok.at[k, fo], worker(fo, th), tg)

    tokens_out(dqh, qt, 0)

    def spread(src, dst, slot, ks, ki):
        for n in range(G):
            p = lax.rem(h + n, G)
            move(n, cols(src, p), rows(dst, slot, FB), sem_send.at[ks], sem_in.at[ki], worker(fo, p), g)

    spread(ckh, ckb, r, 2, 0)
    spread(cvh, cvb, r, 3, 1)

    row = lax.broadcasted_iota(jnp.int32, (FB, HD), 0)
    for blk in range(2 * G):
        gb = f * G - R + blk
        length = len_ref[jnp.clip(gb, 0, NF * G - 1)]
        length = jnp.where((gb >= 0) & (gb < NF * G), length, 0)
        bias[blk * FB:(blk + 1) * FB, :] = jnp.where(row < length, 0.0, NEG).astype(F32)
    zero = jnp.zeros((R * FB, HD), BF16)

    @pl.when(f == 0)
    def _():
        ekb[0:R * FB, :] = zero
        evb[0:R * FB, :] = zero

    @pl.when(f == NF - 1)
    def _():
        ekb[(R + G) * FB:, :] = zero
        evb[(R + G) * FB:, :] = zero

    eka[...] = jnp.zeros(eka.shape, F32)
    eva[...] = jnp.zeros(eva.shape, F32)

    drain(rows(qt, f, TC), sem_tok.at[0, f])
    partner = worker(2 * x + 1 - c, h)

    def same_core(i):
        return 2 * lax.rem(x + i, NX) + c

    def other_core(i):
        return 2 * lax.rem(x + i, NX) + 1 - c

    for n in range(1, NX):
        send(rows(qt, f, TC), rows(qt, f, TC), sem_send.at[10], sem_tok.at[0, f], worker(same_core(n), h), g)
    send(rows(qt, f, TC), rows(qt, f, TC), sem_send.at[29], sem_tok.at[0, f], partner, g)
    spread(ek, ekb, R + r, 4, 2)
    spread(ev, evb, R + r, 5, 3)

    row8 = lax.broadcasted_iota(jnp.int32, (8, TC), 0)

    def pack(a, b, c):
        return jnp.where(row8 == 0, a, jnp.where(row8 == 1, b, c))

    drain(ckb, sem_in.at[0])
    drain(cvb, sem_in.at[1])
    spread(eq, eqb, r, 6, 4)
    spread(ec, ecb, r, 7, 5)
    tokens_out(dch, ct, 1)
    cvT[...] = cvb[...].T
    ckT[...] = ckb[...].T

    def chunk(t):
        return pl.ds(pl.multiple_of(t * TC, TC), TC)

    def cross_forward(t):
        q = qt[chunk(t), :]
        top = None
        for u in range(G // 2):
            part = nt(ckb[u * W:(u + 1) * W, :], q)
            part = part + lanes(bias[(R * FB) + u * W:(R * FB) + (u + 1) * W, :], TC)
            sbuf[u * W:(u + 1) * W, 0:TC] = part
            high = jnp.max(part, axis=0, keepdims=True)
            top = high if top is None else jnp.maximum(top, high)
        total = jnp.zeros((1, TC), F32)
        for u in range(G // 2):
            expo = jnp.exp2((sbuf[u * W:(u + 1) * W, 0:TC] - top) * C2)
            total = total + jnp.sum(expo, axis=0, keepdims=True)
            pbuf[u * W:(u + 1) * W, chunk(t)] = expo.astype(BF16)
        mloc[t] = pack(top, total, total)
        return nn(cvT[...], pbuf[:, chunk(t)])

    numf[x] = cross_forward(f)

    def halo_out(k, ref):
        drain(ref.at[R * FB:(R + G) * FB, :], sem_in.at[2 + k])

        @pl.when(f > 0)
        def _():
            send(
                ref.at[R * FB:2 * R * FB, :], ref.at[(R + G) * FB:(2 * R + G) * FB, :],
                sem_send.at[8 + k], sem_halo.at[k, 0], worker(f - 1, h), g,
            )

        @pl.when(f < NF - 1)
        def _():
            send(
                ref.at[G * FB:(R + G) * FB, :], ref.at[0:R * FB, :],
                sem_send.at[26 + k], sem_halo.at[k, 1], worker(f + 1, h), g,
            )

    @pl.loop(1, NX)
    def _(i):
        t = same_core(i)
        drain(rows(qt, t, TC), sem_tok.at[0, t])
        send(rows(qt, t, TC), rows(qt, t, TC), sem_send.at[29], sem_tok.at[0, t], partner, g)
        numf[lax.rem(x + i, NX)] = cross_forward(t)

    halo_out(0, ekb)
    def for_partner(i):
        t = other_core(i)
        drain(rows(qt, t, TC), sem_tok.at[0, t])
        nsend[t] = cross_forward(t).astype(BF16)
        send(nsend.at[t], npart.at[t], sem_send.at[30], sem_np.at[0, t], partner, g)
        send(mloc.at[t], spart.at[t], sem_send.at[31], sem_np.at[1, t], partner, g)

    @pl.loop(0, NX // 2)
    def _(i):
        for_partner(i)

    halo_out(1, evb)

    @pl.loop(NX // 2, NX)
    def _(i):
        for_partner(i)

    def joined(i):
        t = same_core(i)
        drain(npart.at[t], sem_np.at[0, t])
        drain(spart.at[t], sem_np.at[1, t])
        top = jnp.maximum(mloc[t, 0:1, :], spart[t, 0:1, :])
        mine = jnp.exp2((mloc[t, 0:1, :] - top) * C2)
        theirs = jnp.exp2((spart[t, 0:1, :] - top) * C2)
        total = mine * mloc[t, 1:2, :] + theirs * spart[t, 1:2, :]
        numer = mine * numf[lax.rem(x + i, NX)] + theirs * npart[t].astype(F32)
        return t, numer.astype(BF16), pack(top, total, total)

    @pl.loop(1, NX)
    def _(i):
        t, numer, stats = joined(i)
        nsend[t] = numer
        ssend[t] = stats
        send(nsend.at[t], nrecv.at[x], sem_send.at[12], sem_num, worker(t, h), g)
        send(ssend.at[t], srecv.at[x], sem_send.at[13], sem_st, worker(t, h), g)

    _, nrecv[x], srecv[x] = joined(0)

    def halo_in(k, ref):
        @pl.when(f > 0)
        def _():
            drain(rows(ref, 0, R * FB), sem_halo.at[k, 1])

        @pl.when(f < NF - 1)
        def _():
            drain(rows(ref, 0, R * FB), sem_halo.at[k, 0])

    drain(eqb, sem_in.at[4])
    halo_in(0, ekb)
    ekT[...] = ekb[...].T

    NU = (G + 2) // 2
    urow = lax.broadcasted_iota(jnp.int32, (W, W), 0)
    ulane = lax.broadcasted_iota(jnp.int32, (W, W), 1)

    def home(src, b, dst, ks, ko):
        away = f * G + b

        @pl.when(away != s)
        def _():
            send(rows(src, b, FB), dst.at[:, col], sem_send.at[ks], sem_out.at[ko], away, g)

        @pl.when(away == s)
        def _():
            pltpu.make_async_copy(rows(src, b, FB), dst.at[:, col], sem_out.at[ko]).start()

    def score(j, u, sb):
        at = pl.ds(pl.multiple_of(j * W + u * W, W), W)
        q = eqb[pl.ds(pl.multiple_of(j * W, W), W), :]
        part = nt(ekb[at, :], q) + lanes(bias[at, :], W)
        if u == 0:
            part = jnp.where((urow < FB) & (ulane >= FB), NEG, part)
        if u == NU - 1:
            part = jnp.where((urow >= FB) & (ulane < FB), NEG, part)
        sb[u * W:(u + 1) * W, :] = part
        return jnp.max(part, axis=0, keepdims=True)

    def exponents(top, sb, wb):
        total = jnp.zeros((1, W), F32)
        for u in range(NU):
            expo = jnp.exp2((sb[u * W:(u + 1) * W, :] - top) * C2)
            total = total + jnp.sum(expo, axis=0, keepdims=True)
            sb[u * W:(u + 1) * W, :] = expo
            wb[u * W:(u + 1) * W, :] = expo.astype(BF16)
        return total

    def output(j, total, wb):
        base = pl.multiple_of(j * W, W)
        numer = nn(evT[:, pl.ds(base, NU * W)], wb[...])
        out = (numer / total).astype(BF16).astype(F32)
        delta = jnp.sum(ecb[pl.ds(base, W), :].astype(F32).T * out, axis=0, keepdims=True)
        eos[pl.ds(base, W), :] = out.T.astype(BF16)
        return 1.0 / total, delta

    def gradients(j, u, sb, inv, delta):
        base = pl.multiple_of(j * W, W)
        at = pl.multiple_of(base + u * W, W)
        q = eqb[pl.ds(base, W), :]
        cot = ecb[pl.ds(base, W), :]
        prob = sb[u * W:(u + 1) * W, :] * inv
        dprob = nt(evb[pl.ds(at, W), :], cot)
        ds = (prob * (dprob - delta)).astype(BF16)
        dsbuf[u * W:(u + 1) * W, :] = ds
        eka[pl.ds(at, W), :] += nn(ds, q)
        eva[pl.ds(at, W), :] += nn(prob.astype(BF16), cot)

    def pair_step(j, sb, wb, inv, delta, nj, nsb, nwb):
        base = pl.multiple_of(j * W, W)
        top = None
        for u in range(NU):
            gradients(j, u, sb, inv, delta)
            if nj is not None:
                high = score(nj, u, nsb)
                top = high if top is None else jnp.maximum(top, high)
        dq = nn(ekT[:, pl.ds(base, NU * W)], dsbuf[...]) * SCALE
        edqs[pl.ds(base, W), :] = dq.T.astype(BF16)
        ahead = None
        if nj is not None:
            total = exponents(top, nsb, nwb)
            ahead = output(nj, total, nwb)
        for half in range(2):
            home(eos, 2 * j + half, o_eo, 14, 0)
            home(edqs, 2 * j + half, o_edq, 15, 1)
        return ahead

    def chunk_home(src, dst, k):
        mine = pl.ds(pl.multiple_of((g * G + h) * HD, HD), HD)
        for n in range(2 * G):
            to = lax.rem(place + n, 2 * G)
            tr, tg = lax.div(to, 2), lax.rem(to, 2)
            move(n, rows(src, to, TB), dst.at[:, mine], sem_send.at[k], sem_out.at[k - 12], f * G + tr, tg)

    def combine():
        drain(nrecv.at[0:NX - 1], sem_num)
        drain(srecv.at[0:NX - 1], sem_st)
        top = srecv[0, 0:1, :]
        for n in range(1, NX):
            top = jnp.maximum(top, srecv[n, 0:1, :])
        total = jnp.zeros((1, TC), F32)
        numer = jnp.zeros((HD, TC), F32)
        for n in range(NX):
            share = jnp.exp2((srecv[n, 0:1, :] - top) * C2)
            total = total + share * srecv[n, 1:2, :]
            numer = numer + share * nrecv[n].astype(F32)
        out = (numer / total).astype(BF16).astype(F32)
        delta = jnp.sum(ct[chunk(f), :].astype(F32).T * out, axis=0, keepdims=True)
        toko[...] = out.T.astype(BF16)
        stat[f] = pack(top, 1.0 / total, delta)
        for n in range(1, NF):
            to = lax.rem(f + n, NF)
            send(stat.at[f], stat.at[f], sem_send.at[18], sem_stat.at[f], worker(to, h), g)
        chunk_home(toko, o_do, 16)

    back = lax.rem(z, 2)

    def pair_at(i):
        return i * (1 - back) + (G // 2 - 1 - i) * back

    def rim(side):
        to = f - 1 + 2 * side

        @pl.when((to >= 0) & (to < NF))
        def _():
            edge = pl.ds(pl.multiple_of(side * ((R + G) * FB), R * FB), R * FB)
            gsend[side, 0] = (eka[edge, :] * SCALE).astype(BF16)
            gsend[side, 1] = eva[edge, :].astype(BF16)
            send(gsend.at[side], grecv.at[1 - side], sem_send.at[19 + side], sem_grad.at[1 - side], worker(to, h), g)

    def half_home(half):
        near = f - 1 + 2 * half
        into = pl.ds(pl.multiple_of(half * (R * FB), R * FB), R * FB)
        start = pl.ds(pl.multiple_of((1 + half) * (R * FB), R * FB), R * FB)
        there = (near >= 0) & (near < NF)

        @pl.when(there)
        def _():
            drain(grecv.at[half], sem_grad.at[half])
            edks[into, :] = (eka[start, :] * SCALE + grecv[half, 0].astype(F32)).astype(BF16)
            edvs[into, :] = (eva[start, :] + grecv[half, 1].astype(F32)).astype(BF16)

        @pl.when(jnp.logical_not(there))
        def _():
            edks[into, :] = (eka[start, :] * SCALE).astype(BF16)
            edvs[into, :] = eva[start, :].astype(BF16)

        for n in range(R):
            b = half * R + lax.rem(r + n, R)
            home(edks, b, o_edk, 22, 2)
            home(edvs, b, o_edv, 23, 3)

    slots = ((sbuf, wbuf), (sbuf2, wbuf2))
    top = None
    for u in range(NU):
        high = score(pair_at(0), u, sbuf)
        top = high if top is None else jnp.maximum(top, high)
    total = exponents(top, sbuf, wbuf)
    halo_in(1, evb)
    evT[...] = evb[...].T
    drain(ecb, sem_in.at[5])
    drain(rows(ct, f, TC), sem_tok.at[1, f])
    for n in range(1, NX):
        send(rows(ct, f, TC), rows(ct, f, TC), sem_send.at[11], sem_tok.at[1, f], worker(same_core(n), h), g)
    send(rows(ct, f, TC), rows(ct, f, TC), sem_send.at[32], sem_tok.at[1, f], partner, g)
    ahead = output(pair_at(0), total, wbuf)
    for i in range(G // 2):
        if i == G // 4:
            combine()
            rim(back)
        if i == G // 2 - 1:
            for n in range(1, NX):
                t = same_core(n)
                drain(rows(ct, t, TC), sem_tok.at[1, t])
                send(rows(ct, t, TC), rows(ct, t, TC), sem_send.at[32], sem_tok.at[1, t], partner, g)
        more = i + 1 < G // 2
        ahead = pair_step(
            pair_at(i), *slots[i % 2], *ahead,
            pair_at(i + 1) if more else None, *slots[(i + 1) % 2],
        )

    rim(1 - back)

    def cross_backward(t):
        cot = ct[chunk(t), :]
        share = jnp.exp2((mloc[t, 0:1, :] - stat[t, 0:1, :]) * C2) * stat[t, 1:2, :]
        delta = stat[t, 2:3, :]
        for u in range(G // 2):
            here = slice(u * W, (u + 1) * W)
            prob = pbuf[here, chunk(t)].astype(F32) * share
            dprob = nt(cvb[here, :], cot)
            dbuf[here, chunk(t)] = (prob * (dprob - delta)).astype(BF16)
            pbuf[here, chunk(t)] = prob.astype(BF16)
        return nn(ckT[...], dbuf[:, chunk(t)])

    def backward_step(t):
        drain(stat.at[t], sem_stat.at[t])
        return cross_backward(t)

    order = sorted(range(1, NX), key=lambda i: -min(i, NX - i))

    for i in (*order, 0):
        t = other_core(i)
        drain(rows(ct, t, TC), sem_tok.at[1, t])
        dqsend[t] = backward_step(t).astype(BF16)
        send(dqsend.at[t], dqpart.at[t], sem_send.at[28], sem_part.at[t], partner, g)

    def for_others(i):
        t = same_core(i)
        dq = backward_step(t)
        drain(dqpart.at[t], sem_part.at[t])
        dqsend[t] = (dq + dqpart[t].astype(F32)).astype(BF16)
        send(dqsend.at[t], dqrecv.at[x], sem_send.at[21], sem_dq, worker(t, h), g)

    half_home(1 - back)

    for i in order:
        for_others(i)

    dqown[...] = cross_backward(f)
    half_home(back)

    def cross_grads(n):
        here = pl.ds(pl.multiple_of(lax.rem(z + n, G // 2) * W, W), W)
        cdks[here, :] = (nn(dbuf[here, :], qt[...]) * SCALE).astype(BF16)
        cdvs[here, :] = nn(pbuf[here, :], ct[...]).astype(BF16)

    def cross_home(n):
        u = lax.rem(z + n, G // 2)
        for half in range(2):
            home(cdks, 2 * u + half, o_cdk, 24, 6)
            home(cdvs, 2 * u + half, o_cdv, 25, 7)

    @pl.loop(0, G // 4)
    def _(n):
        cross_grads(n)
        cross_home(n)

    @pl.loop(G // 4, G // 2)
    def _(n):
        cross_grads(n)

    drain(dqpart.at[f], sem_part.at[f])
    drain(dqrecv.at[0:NX - 1], sem_dq)
    dq = dqown[...] + dqpart[f].astype(F32)
    for n in range(1, NX):
        dq = dq + dqrecv[lax.rem(x + n, NX)].astype(F32)
    tokdq[...] = (dq * SCALE).T.astype(BF16)
    chunk_home(tokdq, o_ddq, 17)

    @pl.loop(G // 4, G // 2)
    def _(n):
        cross_home(n)

    def sent(kept, heads, tokens):
        for k in heads:
            drain(eqb.at[0:(G - kept) * FB, :], sem_send.at[k])
        for k in tokens:
            drain(qt.at[0:(2 * G - kept) * TB, :], sem_send.at[k])

    def all_sent(heads, tokens):
        @pl.when(same)
        def _():
            sent(1, heads, tokens)

        @pl.when(split)
        def _():
            sent(0, heads, tokens)

    all_sent((2, 3, 4, 5, 6, 7, 14, 15, 22, 23), (0, 1, 16))
    drain(qt.at[0:(NX - 1) * TC, :], sem_send.at[10])
    drain(qt.at[0:NX * TC, :], sem_send.at[29])
    drain(nsend.at[0:NX], sem_send.at[30])
    drain(stat.at[0:NX], sem_send.at[31])
    drain(qt.at[0:(NX - 1) * TC, :], sem_send.at[11])
    drain(qt.at[0:NX * TC, :], sem_send.at[32])
    drain(nsend.at[0:NX - 1], sem_send.at[12])
    drain(stat.at[0:NX - 1], sem_send.at[13])
    drain(stat.at[0:NF - 1], sem_send.at[18])
    drain(dqrecv.at[0:NX - 1], sem_send.at[21])
    drain(dqrecv.at[0:NX], sem_send.at[28])

    @pl.when(f > 0)
    def _():
        drain(rows(ekb, 0, R * FB), sem_send.at[8])
        drain(rows(evb, 0, R * FB), sem_send.at[9])
        drain(grecv.at[0], sem_send.at[19])

    @pl.when(f < NF - 1)
    def _():
        drain(rows(ekb, 0, R * FB), sem_send.at[26])
        drain(rows(evb, 0, R * FB), sem_send.at[27])
        drain(grecv.at[1], sem_send.at[20])

    all_sent((24, 25), (17,))
    for k, ref in enumerate((o_eo, o_edq, o_edk, o_edv, o_do, o_ddq, o_cdk, o_cdv)):
        drain(ref, sem_out.at[k])


def finish(*refs):
    n = 8
    sources, results, held, sems = refs[:n], refs[n:2 * n], refs[2 * n:3 * n], refs[3 * n]
    for k in range(n):
        pltpu.make_async_copy(sources[k], held[k], sems.at[0, k]).start()
    for k in range(n):
        pltpu.make_async_copy(sources[k], held[k], sems.at[0, k]).wait()
        pltpu.make_async_copy(held[k], results[k], sems.at[1, k]).start()
    for k in range(n):
        pltpu.make_async_copy(held[k], results[k], sems.at[1, k]).wait()


def local(enc_q, enc_k, enc_v, enc_cot, cross_k, cross_v, dec_q, dec_cot, frame_lengths):
    G = enc_q.shape[1] // HD
    NF = lax.axis_size("seq") // G
    R = G // 2
    NX = NF // 2
    TC = 2 * TB * G
    NW = (G + 2) * FB
    frames = jax.ShapeDtypeStruct(enc_q.shape, BF16)
    tokens = jax.ShapeDtypeStruct(dec_q.shape, BF16)
    any_spec = pl.BlockSpec(memory_space=pl.ANY)
    v = pltpu.VMEM
    scratch = [
        v((G * FB, HD), BF16), v((G * FB, HD), BF16),
        v((2 * G * FB, HD), BF16), v((2 * G * FB, HD), BF16),
        v((HD, 2 * G * FB), BF16), v((HD, 2 * G * FB), BF16),
        v((G * FB, HD), BF16), v((G * FB, HD), BF16),
        v((HD, G * FB), BF16), v((HD, G * FB), BF16),
        v((NF * TC, HD), BF16), v((NF * TC, HD), BF16),
        v((G * FB, NF * TC), BF16), v((G * FB, NF * TC), BF16),
        v((NW, 2 * FB), F32), v((NW, 2 * FB), F32),
        v((NW, 2 * FB), BF16), v((NW, 2 * FB), BF16), v((NW, 2 * FB), BF16),
        v((2 * G * FB, HD), F32),
        v((NF, HD, TC), BF16), v((NX, HD, TC), BF16),
        v((NF, HD, TC), BF16), v((NX, HD, TC), F32),
        v((NF, 8, TC), F32), v((NX, 8, TC), F32), v((NF, 8, TC), F32),
        v((NF, 8, TC), F32), v((NF, 8, TC), F32),
        v((NF, HD, TC), BF16), v((NX, HD, TC), BF16),
        v((NF, HD, TC), BF16), v((HD, TC), F32),
        v((G * FB, HD), BF16), v((G * FB, HD), BF16),
        v((G * FB, HD), BF16), v((G * FB, HD), BF16),
        v((2 * G * FB, HD), F32), v((2 * G * FB, HD), F32),
        v((2, 2, R * FB, HD), BF16), v((2, 2, R * FB, HD), BF16),
        v((G * FB, HD), BF16), v((G * FB, HD), BF16),
        v((TC, HD), BF16), v((TC, HD), BF16),
        pltpu.SemaphoreType.DMA((6,)),
        pltpu.SemaphoreType.DMA((2, 2)),
        pltpu.SemaphoreType.DMA((2, NF)),
        pltpu.SemaphoreType.DMA((2, NF)),
        pltpu.SemaphoreType.DMA(()),
        pltpu.SemaphoreType.DMA(()),
        pltpu.SemaphoreType.DMA((NF,)),
        pltpu.SemaphoreType.DMA(()),
        pltpu.SemaphoreType.DMA((NF,)),
        pltpu.SemaphoreType.DMA((2,)),
        pltpu.SemaphoreType.DMA((8,)),
        pltpu.SemaphoreType.DMA((33,)),
    ]
    shapes = (frames, frames, frames, frames, tokens, tokens, frames, frames)
    staged = pl.pallas_call(
        functools.partial(kernel, G, NF),
        out_shape=shapes,
        in_specs=[pl.BlockSpec(memory_space=pltpu.SMEM)] + [any_spec] * 8,
        out_specs=(any_spec,) * 8,
        scratch_shapes=scratch,
        compiler_params=pltpu.CompilerParams(
            collective_id=0, has_side_effects=True, vmem_limit_bytes=VMEM_ALL
        ),
    )(frame_lengths, enc_q, enc_k, enc_v, enc_cot, cross_k, cross_v, dec_q, dec_cot)
    return pl.pallas_call(
        finish,
        out_shape=shapes,
        in_specs=[any_spec] * 8,
        out_specs=(any_spec,) * 8,
        scratch_shapes=[v(item.shape, BF16) for item in shapes] + [pltpu.SemaphoreType.DMA((2, 8))],
        compiler_params=pltpu.CompilerParams(vmem_limit_bytes=VMEM_ALL),
    )(*staged)


def solution(mesh):
    frames = P("seq", "grp")
    tokens = P(("seq", "grp"), None)
    return jax.shard_map(
        local,
        mesh=mesh,
        in_specs=(frames,) * 6 + (tokens,) * 2 + (P(),),
        out_specs=(frames,) * 4 + (tokens,) * 2 + (frames,) * 2,
        check_vma=False,
    )
```

```python
import functools
import math

import jax
import jax.numpy as jnp
from jax import lax
from jax.experimental import pallas as pl
from jax.experimental.pallas import tpu as pltpu
from jax.sharding import PartitionSpec as P

HD = 128
FB = 128
TB = 16
SCALE = HD ** (-0.5)
C2 = SCALE * math.log2(math.e)
NEG = -1e30
F32 = jnp.float32
BF16 = jnp.bfloat16
MESH = pl.DeviceIdType.MESH
VMEM_ALL = 67043328


def nt(a, b):
    return lax.dot_general(a, b, (((1,), (1,)), ((), ())), preferred_element_type=F32)


def nn(a, b):
    return lax.dot_general(a, b, (((1,), (0,)), ((), ())), preferred_element_type=F32)


def drain(ref, sem):
    pltpu.make_async_copy(ref, ref, sem).wait()


def lanes(column, width):
    return column if width == HD else jnp.concatenate([column] * (width // HD), axis=1)


def kernel(
    G, NF, len_ref, eq, ek, ev, ec, ckh, cvh, dqh, dch,
    o_eo, o_edq, o_edk, o_edv, o_do, o_ddq, o_cdk, o_cdv,
    eqb, ecb, ekb, evb, ekT, evT, ckb, cvb, ckT, cvT, qt, ct, pbuf, dbuf, sbuf, sbuf2, wbuf, wbuf2, dsbuf,
    bias, nsend, nrecv, npart, numf, ssend, srecv, spart, mloc, stat, dqsend, dqrecv, dqpart, dqown,
    eos, edqs, edks, edvs, eka, eva, gsend, grecv, cdks, cdvs, toko, tokdq,
    sem_in, sem_halo, sem_tok, sem_np, sem_num, sem_st, sem_stat, sem_dq, sem_part, sem_grad, sem_out, sem_send,
):
    R = G // 2
    NX = NF // 2
    TC = 2 * TB * G
    W = 2 * FB
    s = lax.axis_index("seq")
    g = lax.axis_index("grp")
    fo = lax.div(s, G)
    r = lax.rem(s, G)
    x, yl = lax.div(fo, 2), lax.rem(fo, 2)
    z, c = lax.div(r, 2), lax.rem(r, 2)
    f = 2 * x + c
    h = yl * R + z
    same = yl == c
    split = yl != c
    col = pl.ds(pl.multiple_of(h * HD, HD), HD)

    def worker(group, head):
        return (lax.div(group, 2) * 2 + lax.div(head, R)) * G + lax.rem(head, R) * 2 + lax.rem(group, 2)

    def send(src, dst, ssem, rsem, ts, tg):
        pltpu.make_async_remote_copy(
            src_ref=src, dst_ref=dst, send_sem=ssem, recv_sem=rsem,
            device_id=(ts, tg), device_id_type=MESH,
        ).start()

    def move(n, src, dst, ssem, rsem, ts, tg):
        if n > 0:
            send(src, dst, ssem, rsem, ts, tg)
            return

        @pl.when(same)
        def _():
            pltpu.make_async_copy(src, dst, rsem).start()

        @pl.when(split)
        def _():
            send(src, dst, ssem, rsem, ts, tg)

    def cols(ref, head):
        return ref.at[:, pl.ds(pl.multiple_of(head * HD, HD), HD)]

    def rows(ref, index, size):
        return ref.at[pl.ds(pl.multiple_of(index * size, size), size), :]

    barrier = pltpu.get_barrier_semaphore()

    def greet(ts, tg):
        pl.semaphore_signal(barrier, inc=1, device_id=(ts, tg), device_id_type=MESH)

    for n in range(1, NF):
        greet(worker(lax.rem(f + n, NF), h), g)
    for n in range(G):
        greet(worker(fo, lax.rem(h + n, G)), 1 - g)
        greet(f * G + lax.rem(r + n, G), 1 - g)
    for n in range(1, G):
        greet(worker(fo, lax.rem(h + n, G)), g)
        greet(f * G + lax.rem(r + n, G), g)

    @pl.when(split)
    def _():
        greet(worker(fo, h), g)
        greet(f * G + r, g)

    pl.semaphore_wait(barrier, 4 * G + NF - 1 - 2 * jnp.where(same, 1, 0))

    place = r * 2 + g
    own_tok = fo * (2 * G) + place

    def tokens_out(src, dst, k):
        for n in range(2 * G):
            to = lax.rem(h * 2 + g + n, 2 * G)
            th, tg = lax.div(to, 2), lax.rem(to, 2)
            move(n, cols(src, tg * G + th), rows(dst, own_tok, TB), sem_send.at[k], sem_tok.at[k, fo], worker(fo, th), tg)

    tokens_out(dqh, qt, 0)

    def spread(src, dst, slot, ks, ki):
        for n in range(G):
            p = lax.rem(h + n, G)
            move(n, cols(src, p), rows(dst, slot, FB), sem_send.at[ks], sem_in.at[ki], worker(fo, p), g)

    spread(ckh, ckb, r, 2, 0)
    spread(cvh, cvb, r, 3, 1)

    row = lax.broadcasted_iota(jnp.int32, (FB, HD), 0)
    for blk in range(2 * G):
        gb = f * G - R + blk
        length = len_ref[jnp.clip(gb, 0, NF * G - 1)]
        length = jnp.where((gb >= 0) & (gb < NF * G), length, 0)
        bias[blk * FB:(blk + 1) * FB, :] = jnp.where(row < length, 0.0, NEG).astype(F32)
    zero = jnp.zeros((R * FB, HD), BF16)

    @pl.when(f == 0)
    def _():
        ekb[0:R * FB, :] = zero
        evb[0:R * FB, :] = zero

    @pl.when(f == NF - 1)
    def _():
        ekb[(R + G) * FB:, :] = zero
        evb[(R + G) * FB:, :] = zero

    eka[...] = jnp.zeros(eka.shape, F32)
    eva[...] = jnp.zeros(eva.shape, F32)

    drain(rows(qt, f, TC), sem_tok.at[0, f])
    partner = worker(2 * x + 1 - c, h)

    def same_core(i):
        return 2 * lax.rem(x + i, NX) + c

    def other_core(i):
        return 2 * lax.rem(x + i, NX) + 1 - c

    for n in range(1, NX):
        send(rows(qt, f, TC), rows(qt, f, TC), sem_send.at[10], sem_tok.at[0, f], worker(same_core(n), h), g)
    send(rows(qt, f, TC), rows(qt, f, TC), sem_send.at[29], sem_tok.at[0, f], partner, g)
    spread(ek, ekb, R + r, 4, 2)
    spread(ev, evb, R + r, 5, 3)

    row8 = lax.broadcasted_iota(jnp.int32, (8, TC), 0)

    def pack(a, b, c):
        return jnp.where(row8 == 0, a, jnp.where(row8 == 1, b, c))

    drain(ckb, sem_in.at[0])
    drain(cvb, sem_in.at[1])
    spread(eq, eqb, r, 6, 4)
    spread(ec, ecb, r, 7, 5)
    tokens_out(dch, ct, 1)
    cvT[...] = cvb[...].T
    ckT[...] = ckb[...].T

    def chunk(t):
        return pl.ds(pl.multiple_of(t * TC, TC), TC)

    def cross_forward(t):
        q = qt[chunk(t), :]
        top = None
        for u in range(G // 2):
            part = nt(ckb[u * W:(u + 1) * W, :], q)
            part = part + lanes(bias[(R * FB) + u * W:(R * FB) + (u + 1) * W, :], TC)
            sbuf[u * W:(u + 1) * W, 0:TC] = part
            high = jnp.max(part, axis=0, keepdims=True)
            top = high if top is None else jnp.maximum(top, high)
        total = jnp.zeros((1, TC), F32)
        for u in range(G // 2):
            expo = jnp.exp2((sbuf[u * W:(u + 1) * W, 0:TC] - top) * C2)
            total = total + jnp.sum(expo, axis=0, keepdims=True)
            pbuf[u * W:(u + 1) * W, chunk(t)] = expo.astype(BF16)
        mloc[t] = pack(top, total, total)
        return nn(cvT[...], pbuf[:, chunk(t)])

    numf[x] = cross_forward(f)

    def halo_out(k, ref):
        drain(ref.at[R * FB:(R + G) * FB, :], sem_in.at[2 + k])

        @pl.when(f > 0)
        def _():
            send(
                ref.at[R * FB:2 * R * FB, :], ref.at[(R + G) * FB:(2 * R + G) * FB, :],
                sem_send.at[8 + k], sem_halo.at[k, 0], worker(f - 1, h), g,
            )

        @pl.when(f < NF - 1)
        def _():
            send(
                ref.at[G * FB:(R + G) * FB, :], ref.at[0:R * FB, :],
                sem_send.at[26 + k], sem_halo.at[k, 1], worker(f + 1, h), g,
            )

    @pl.loop(1, NX)
    def _(i):
        t = same_core(i)
        drain(rows(qt, t, TC), sem_tok.at[0, t])
        send(rows(qt, t, TC), rows(qt, t, TC), sem_send.at[29], sem_tok.at[0, t], partner, g)
        numf[lax.rem(x + i, NX)] = cross_forward(t)

    halo_out(0, ekb)
    def for_partner(i):
        t = other_core(i)
        drain(rows(qt, t, TC), sem_tok.at[0, t])
        nsend[t] = cross_forward(t).astype(BF16)
        send(nsend.at[t], npart.at[t], sem_send.at[30], sem_np.at[0, t], partner, g)
        send(mloc.at[t], spart.at[t], sem_send.at[31], sem_np.at[1, t], partner, g)

    @pl.loop(0, NX // 2)
    def _(i):
        for_partner(i)

    halo_out(1, evb)

    @pl.loop(NX // 2, NX)
    def _(i):
        for_partner(i)

    def joined(i):
        t = same_core(i)
        drain(npart.at[t], sem_np.at[0, t])
        drain(spart.at[t], sem_np.at[1, t])
        top = jnp.maximum(mloc[t, 0:1, :], spart[t, 0:1, :])
        mine = jnp.exp2((mloc[t, 0:1, :] - top) * C2)
        theirs = jnp.exp2((spart[t, 0:1, :] - top) * C2)
        total = mine * mloc[t, 1:2, :] + theirs * spart[t, 1:2, :]
        numer = mine * numf[lax.rem(x + i, NX)] + theirs * npart[t].astype(F32)
        return t, numer.astype(BF16), pack(top, total, total)

    @pl.loop(1, NX)
    def _(i):
        t, numer, stats = joined(i)
        nsend[t] = numer
        ssend[t] = stats
        send(nsend.at[t], nrecv.at[x], sem_send.at[12], sem_num, worker(t, h), g)
        send(ssend.at[t], srecv.at[x], sem_send.at[13], sem_st, worker(t, h), g)

    _, nrecv[x], srecv[x] = joined(0)

    def halo_in(k, ref):
        @pl.when(f > 0)
        def _():
            drain(rows(ref, 0, R * FB), sem_halo.at[k, 1])

        @pl.when(f < NF - 1)
        def _():
            drain(rows(ref, 0, R * FB), sem_halo.at[k, 0])

    drain(eqb, sem_in.at[4])
    halo_in(0, ekb)
    ekT[...] = ekb[...].T

    NU = (G + 2) // 2
    urow = lax.broadcasted_iota(jnp.int32, (W, W), 0)
    ulane = lax.broadcasted_iota(jnp.int32, (W, W), 1)

    def home(src, b, dst, ks, ko):
        away = f * G + b

        @pl.when(away != s)
        def _():
            send(rows(src, b, FB), dst.at[:, col], sem_send.at[ks], sem_out.at[ko], away, g)

        @pl.when(away == s)
        def _():
            pltpu.make_async_copy(rows(src, b, FB), dst.at[:, col], sem_out.at[ko]).start()

    def score(j, u, sb):
        at = pl.ds(pl.multiple_of(j * W + u * W, W), W)
        q = eqb[pl.ds(pl.multiple_of(j * W, W), W), :]
        part = nt(ekb[at, :], q) + lanes(bias[at, :], W)
        if u == 0:
            part = jnp.where((urow < FB) & (ulane >= FB), NEG, part)
        if u == NU - 1:
            part = jnp.where((urow >= FB) & (ulane < FB), NEG, part)
        sb[u * W:(u + 1) * W, :] = part
        return jnp.max(part, axis=0, keepdims=True)

    def exponents(top, sb, wb):
        total = jnp.zeros((1, W), F32)
        for u in range(NU):
            expo = jnp.exp2((sb[u * W:(u + 1) * W, :] - top) * C2)
            total = total + jnp.sum(expo, axis=0, keepdims=True)
            sb[u * W:(u + 1) * W, :] = expo
            wb[u * W:(u + 1) * W, :] = expo.astype(BF16)
        return total

    def output(j, total, wb):
        base = pl.multiple_of(j * W, W)
        numer = nn(evT[:, pl.ds(base, NU * W)], wb[...])
        out = (numer / total).astype(BF16).astype(F32)
        delta = jnp.sum(ecb[pl.ds(base, W), :].astype(F32).T * out, axis=0, keepdims=True)
        eos[pl.ds(base, W), :] = out.T.astype(BF16)
        return 1.0 / total, delta

    def gradients(j, u, sb, inv, delta):
        base = pl.multiple_of(j * W, W)
        at = pl.multiple_of(base + u * W, W)
        q = eqb[pl.ds(base, W), :]
        cot = ecb[pl.ds(base, W), :]
        prob = sb[u * W:(u + 1) * W, :] * inv
        dprob = nt(evb[pl.ds(at, W), :], cot)
        ds = (prob * (dprob - delta)).astype(BF16)
        dsbuf[u * W:(u + 1) * W, :] = ds
        eka[pl.ds(at, W), :] += nn(ds, q)
        eva[pl.ds(at, W), :] += nn(prob.astype(BF16), cot)

    def pair_step(j, sb, wb, inv, delta, nj, nsb, nwb, known):
        base = pl.multiple_of(j * W, W)
        top = None
        for u in range(NU):
            gradients(j, u, sb, inv, delta)
            if nj is not None and known is None:
                high = score(nj, u, nsb)
                top = high if top is None else jnp.maximum(top, high)
        dq = nn(ekT[:, pl.ds(base, NU * W)], dsbuf[...]) * SCALE
        edqs[pl.ds(base, W), :] = dq.T.astype(BF16)
        ahead = None
        if nj is not None:
            total = exponents(top, nsb, nwb) if known is None else known
            ahead = output(nj, total, nwb)
        for half in range(2):
            home(eos, 2 * j + half, o_eo, 14, 0)
            home(edqs, 2 * j + half, o_edq, 15, 1)
        return ahead

    def chunk_home(src, dst, k):
        mine = pl.ds(pl.multiple_of((g * G + h) * HD, HD), HD)
        for n in range(2 * G):
            to = lax.rem(place + n, 2 * G)
            tr, tg = lax.div(to, 2), lax.rem(to, 2)
            move(n, rows(src, to, TB), dst.at[:, mine], sem_send.at[k], sem_out.at[k - 12], f * G + tr, tg)

    def combine():
        drain(nrecv.at[0:NX - 1], sem_num)
        drain(srecv.at[0:NX - 1], sem_st)
        top = srecv[0, 0:1, :]
        for n in range(1, NX):
            top = jnp.maximum(top, srecv[n, 0:1, :])
        total = jnp.zeros((1, TC), F32)
        numer = jnp.zeros((HD, TC), F32)
        for n in range(NX):
            share = jnp.exp2((srecv[n, 0:1, :] - top) * C2)
            total = total + share * srecv[n, 1:2, :]
            numer = numer + share * nrecv[n].astype(F32)
        out = (numer / total).astype(BF16).astype(F32)
        delta = jnp.sum(ct[chunk(f), :].astype(F32).T * out, axis=0, keepdims=True)
        toko[...] = out.T.astype(BF16)
        stat[f] = pack(top, 1.0 / total, delta)
        for n in range(1, NF):
            to = lax.rem(f + n, NF)
            send(stat.at[f], stat.at[f], sem_send.at[18], sem_stat.at[f], worker(to, h), g)
        chunk_home(toko, o_do, 16)

    back = lax.rem(z, 2)

    def pair_at(i):
        return i * (1 - back) + (G // 2 - 1 - i) * back

    def rim(side):
        to = f - 1 + 2 * side

        @pl.when((to >= 0) & (to < NF))
        def _():
            edge = pl.ds(pl.multiple_of(side * ((R + G) * FB), R * FB), R * FB)
            gsend[side, 0] = (eka[edge, :] * SCALE).astype(BF16)
            gsend[side, 1] = eva[edge, :].astype(BF16)
            send(gsend.at[side], grecv.at[1 - side], sem_send.at[19 + side], sem_grad.at[1 - side], worker(to, h), g)

    def half_home(half):
        near = f - 1 + 2 * half
        into = pl.ds(pl.multiple_of(half * (R * FB), R * FB), R * FB)
        start = pl.ds(pl.multiple_of((1 + half) * (R * FB), R * FB), R * FB)
        there = (near >= 0) & (near < NF)

        @pl.when(there)
        def _():
            drain(grecv.at[half], sem_grad.at[half])
            edks[into, :] = (eka[start, :] * SCALE + grecv[half, 0].astype(F32)).astype(BF16)
            edvs[into, :] = (eva[start, :] + grecv[half, 1].astype(F32)).astype(BF16)

        @pl.when(jnp.logical_not(there))
        def _():
            edks[into, :] = (eka[start, :] * SCALE).astype(BF16)
            edvs[into, :] = eva[start, :].astype(BF16)

        for n in range(R):
            b = half * R + lax.rem(r + n, R)
            home(edks, b, o_edk, 22, 2)
            home(edvs, b, o_edv, 23, 3)

    slots = ((sbuf, wbuf), (sbuf2, wbuf2))
    top = None
    for u in range(NU):
        high = score(pair_at(0), u, sbuf)
        top = high if top is None else jnp.maximum(top, high)
    total = exponents(top, sbuf, wbuf)
    top = None
    for u in range(NU):
        high = score(pair_at(1), u, sbuf2)
        top = high if top is None else jnp.maximum(top, high)
    second = exponents(top, sbuf2, wbuf2)
    halo_in(1, evb)
    evT[...] = evb[...].T
    drain(ecb, sem_in.at[5])
    ahead = output(pair_at(0), total, wbuf)
    drain(rows(ct, f, TC), sem_tok.at[1, f])
    for n in range(1, NX):
        send(rows(ct, f, TC), rows(ct, f, TC), sem_send.at[11], sem_tok.at[1, f], worker(same_core(n), h), g)
    send(rows(ct, f, TC), rows(ct, f, TC), sem_send.at[32], sem_tok.at[1, f], partner, g)
    for i in range(G // 2):
        if i == G // 4:
            combine()
            rim(back)
        if i == G // 2 - 1:
            for n in range(1, NX):
                t = same_core(n)
                drain(rows(ct, t, TC), sem_tok.at[1, t])
                send(rows(ct, t, TC), rows(ct, t, TC), sem_send.at[32], sem_tok.at[1, t], partner, g)
        more = i + 1 < G // 2
        ahead = pair_step(
            pair_at(i), *slots[i % 2], *ahead,
            pair_at(i + 1) if more else None, *slots[(i + 1) % 2], second if i == 0 else None,
        )

    rim(1 - back)

    def cross_backward(t):
        cot = ct[chunk(t), :]
        share = jnp.exp2((mloc[t, 0:1, :] - stat[t, 0:1, :]) * C2) * stat[t, 1:2, :]
        delta = stat[t, 2:3, :]
        for u in range(G // 2):
            here = slice(u * W, (u + 1) * W)
            prob = pbuf[here, chunk(t)].astype(F32) * share
            dprob = nt(cvb[here, :], cot)
            dbuf[here, chunk(t)] = (prob * (dprob - delta)).astype(BF16)
            pbuf[here, chunk(t)] = prob.astype(BF16)
        return nn(ckT[...], dbuf[:, chunk(t)])

    def backward_step(t):
        drain(stat.at[t], sem_stat.at[t])
        return cross_backward(t)

    order = sorted(range(1, NX), key=lambda i: -min(i, NX - i))

    for i in (*order, 0):
        t = other_core(i)
        drain(rows(ct, t, TC), sem_tok.at[1, t])
        dqsend[t] = backward_step(t).astype(BF16)
        send(dqsend.at[t], dqpart.at[t], sem_send.at[28], sem_part.at[t], partner, g)

    def for_others(i):
        t = same_core(i)
        dq = backward_step(t)
        drain(dqpart.at[t], sem_part.at[t])
        dqsend[t] = (dq + dqpart[t].astype(F32)).astype(BF16)
        send(dqsend.at[t], dqrecv.at[x], sem_send.at[21], sem_dq, worker(t, h), g)

    half_home(1 - back)

    for i in order:
        for_others(i)

    dqown[...] = cross_backward(f)
    half_home(back)

    def cross_grads(n):
        here = pl.ds(pl.multiple_of(lax.rem(z + n, G // 2) * W, W), W)
        cdks[here, :] = (nn(dbuf[here, :], qt[...]) * SCALE).astype(BF16)
        cdvs[here, :] = nn(pbuf[here, :], ct[...]).astype(BF16)

    def cross_home(n):
        u = lax.rem(z + n, G // 2)
        for half in range(2):
            home(cdks, 2 * u + half, o_cdk, 24, 6)
            home(cdvs, 2 * u + half, o_cdv, 25, 7)

    @pl.loop(0, G // 4)
    def _(n):
        cross_grads(n)
        cross_home(n)

    @pl.loop(G // 4, G // 2)
    def _(n):
        cross_grads(n)

    drain(dqpart.at[f], sem_part.at[f])
    drain(dqrecv.at[0:NX - 1], sem_dq)
    dq = dqown[...] + dqpart[f].astype(F32)
    for n in range(1, NX):
        dq = dq + dqrecv[lax.rem(x + n, NX)].astype(F32)
    tokdq[...] = (dq * SCALE).T.astype(BF16)
    chunk_home(tokdq, o_ddq, 17)

    @pl.loop(G // 4, G // 2)
    def _(n):
        cross_home(n)

    def sent(kept, heads, tokens):
        for k in heads:
            drain(eqb.at[0:(G - kept) * FB, :], sem_send.at[k])
        for k in tokens:
            drain(qt.at[0:(2 * G - kept) * TB, :], sem_send.at[k])

    def all_sent(heads, tokens):
        @pl.when(same)
        def _():
            sent(1, heads, tokens)

        @pl.when(split)
        def _():
            sent(0, heads, tokens)

    all_sent((2, 3, 4, 5, 6, 7, 14, 15, 22, 23), (0, 1, 16))
    drain(qt.at[0:(NX - 1) * TC, :], sem_send.at[10])
    drain(qt.at[0:NX * TC, :], sem_send.at[29])
    drain(nsend.at[0:NX], sem_send.at[30])
    drain(stat.at[0:NX], sem_send.at[31])
    drain(qt.at[0:(NX - 1) * TC, :], sem_send.at[11])
    drain(qt.at[0:NX * TC, :], sem_send.at[32])
    drain(nsend.at[0:NX - 1], sem_send.at[12])
    drain(stat.at[0:NX - 1], sem_send.at[13])
    drain(stat.at[0:NF - 1], sem_send.at[18])
    drain(dqrecv.at[0:NX - 1], sem_send.at[21])
    drain(dqrecv.at[0:NX], sem_send.at[28])

    @pl.when(f > 0)
    def _():
        drain(rows(ekb, 0, R * FB), sem_send.at[8])
        drain(rows(evb, 0, R * FB), sem_send.at[9])
        drain(grecv.at[0], sem_send.at[19])

    @pl.when(f < NF - 1)
    def _():
        drain(rows(ekb, 0, R * FB), sem_send.at[26])
        drain(rows(evb, 0, R * FB), sem_send.at[27])
        drain(grecv.at[1], sem_send.at[20])

    all_sent((24, 25), (17,))
    for k, ref in enumerate((o_eo, o_edq, o_edk, o_edv, o_do, o_ddq, o_cdk, o_cdv)):
        drain(ref, sem_out.at[k])


def finish(*refs):
    n = 8
    sources, results, held, sems = refs[:n], refs[n:2 * n], refs[2 * n:3 * n], refs[3 * n]
    for k in range(n):
        pltpu.make_async_copy(sources[k], held[k], sems.at[0, k]).start()
    for k in range(n):
        pltpu.make_async_copy(sources[k], held[k], sems.at[0, k]).wait()
        pltpu.make_async_copy(held[k], results[k], sems.at[1, k]).start()
    for k in range(n):
        pltpu.make_async_copy(held[k], results[k], sems.at[1, k]).wait()


def local(enc_q, enc_k, enc_v, enc_cot, cross_k, cross_v, dec_q, dec_cot, frame_lengths):
    G = enc_q.shape[1] // HD
    NF = lax.axis_size("seq") // G
    R = G // 2
    NX = NF // 2
    TC = 2 * TB * G
    NW = (G + 2) * FB
    frames = jax.ShapeDtypeStruct(enc_q.shape, BF16)
    tokens = jax.ShapeDtypeStruct(dec_q.shape, BF16)
    any_spec = pl.BlockSpec(memory_space=pl.ANY)
    v = pltpu.VMEM
    scratch = [
        v((G * FB, HD), BF16), v((G * FB, HD), BF16),
        v((2 * G * FB, HD), BF16), v((2 * G * FB, HD), BF16),
        v((HD, 2 * G * FB), BF16), v((HD, 2 * G * FB), BF16),
        v((G * FB, HD), BF16), v((G * FB, HD), BF16),
        v((HD, G * FB), BF16), v((HD, G * FB), BF16),
        v((NF * TC, HD), BF16), v((NF * TC, HD), BF16),
        v((G * FB, NF * TC), BF16), v((G * FB, NF * TC), BF16),
        v((NW, 2 * FB), F32), v((NW, 2 * FB), F32),
        v((NW, 2 * FB), BF16), v((NW, 2 * FB), BF16), v((NW, 2 * FB), BF16),
        v((2 * G * FB, HD), F32),
        v((NF, HD, TC), BF16), v((NX, HD, TC), BF16),
        v((NF, HD, TC), BF16), v((NX, HD, TC), F32),
        v((NF, 8, TC), F32), v((NX, 8, TC), F32), v((NF, 8, TC), F32),
        v((NF, 8, TC), F32), v((NF, 8, TC), F32),
        v((NF, HD, TC), BF16), v((NX, HD, TC), BF16),
        v((NF, HD, TC), BF16), v((HD, TC), F32),
        v((G * FB, HD), BF16), v((G * FB, HD), BF16),
        v((G * FB, HD), BF16), v((G * FB, HD), BF16),
        v((2 * G * FB, HD), F32), v((2 * G * FB, HD), F32),
        v((2, 2, R * FB, HD), BF16), v((2, 2, R * FB, HD), BF16),
        v((G * FB, HD), BF16), v((G * FB, HD), BF16),
        v((TC, HD), BF16), v((TC, HD), BF16),
        pltpu.SemaphoreType.DMA((6,)),
        pltpu.SemaphoreType.DMA((2, 2)),
        pltpu.SemaphoreType.DMA((2, NF)),
        pltpu.SemaphoreType.DMA((2, NF)),
        pltpu.SemaphoreType.DMA(()),
        pltpu.SemaphoreType.DMA(()),
        pltpu.SemaphoreType.DMA((NF,)),
        pltpu.SemaphoreType.DMA(()),
        pltpu.SemaphoreType.DMA((NF,)),
        pltpu.SemaphoreType.DMA((2,)),
        pltpu.SemaphoreType.DMA((8,)),
        pltpu.SemaphoreType.DMA((33,)),
    ]
    shapes = (frames, frames, frames, frames, tokens, tokens, frames, frames)
    staged = pl.pallas_call(
        functools.partial(kernel, G, NF),
        out_shape=shapes,
        in_specs=[pl.BlockSpec(memory_space=pltpu.SMEM)] + [any_spec] * 8,
        out_specs=(any_spec,) * 8,
        scratch_shapes=scratch,
        compiler_params=pltpu.CompilerParams(
            collective_id=0, has_side_effects=True, vmem_limit_bytes=VMEM_ALL
        ),
    )(frame_lengths, enc_q, enc_k, enc_v, enc_cot, cross_k, cross_v, dec_q, dec_cot)
    return pl.pallas_call(
        finish,
        out_shape=shapes,
        in_specs=[any_spec] * 8,
        out_specs=(any_spec,) * 8,
        scratch_shapes=[v(item.shape, BF16) for item in shapes] + [pltpu.SemaphoreType.DMA((2, 8))],
        compiler_params=pltpu.CompilerParams(vmem_limit_bytes=VMEM_ALL),
    )(*staged)


def solution(mesh):
    frames = P("seq", "grp")
    tokens = P(("seq", "grp"), None)
    return jax.shard_map(
        local,
        mesh=mesh,
        in_specs=(frames,) * 6 + (tokens,) * 2 + (P(),),
        out_specs=(frames,) * 4 + (tokens,) * 2 + (frames,) * 2,
        check_vma=False,
    )
```
